128 devices in a mesh: slab: 4 (over x), tile: 32 (over y, z, core).
Axes of the slice: x: 4, y: 4, z: 4, core: 2. Of those that a mesh axis runs over, the one named last changes fastest.
Arguments:
- features: bfloat16 [262144, 128], P(('slab', 'tile')), may hold values from -6 to 6
- conv_weight: bfloat16 [27, 128, 128], replicated, may hold values from -0.15625 to 0.15625
- down_weight: bfloat16 [8, 128, 128], replicated, may hold values from -0.25 to 0.25
- coarse_grad: bfloat16 [65536, 128], P(('slab', 'tile')), may hold values from -6 to 6
- rulebook: int32 [27, 262144], P(None, ('slab', 'tile')), may hold values from 0 to 3072, as said below
- boundary_rows: int32 [512, 256], P(('slab', 'tile')), may hold values from 0 to 2047, as said below
- parent_code: int32 [262144], P(('slab', 'tile')), may hold values from 0 to 4096, as said below
Outputs:
- coarse: bfloat16 [65536, 128], P(('slab', 'tile'))
- input_grad: float32 [262144, 128], P(('slab', 'tile'))
- conv_grad: float32 [27, 128, 128], replicated
- down_grad: float32 [8, 128, 128], replicated
The draws below stay inside these ranges and needn't reach their ends.
Inputs may be any that keep to these rules, and one draw needn't show every extreme that they name: `rulebook`: each partition has some number of live blocks of 128 rows, at least one and fewer than 16, at its start; rows of the remaining blocks are dead. For a live row, the centre offset (13) reads the row itself; other entries read a live local row, a received row (2048 to 3071) or the empty row 3072. For each offset and each aligned block of 128 rows of a partition, all entries other than 3072 lie in one aligned block of 128 rows of the extended table. Every entry of a dead row is 3072. `boundary_rows`: entries are live rows of the partition; repeats may occur. `parent_code`: within a partition the live rows with one parent have distinct child positions, at most 4 per parent; the parents of the rows of local block b lie in coarse rows b * 32 to (b + 1) * 32 - 1; dead rows have the code 8 * 512.
All inputs are finite; a program needn't handle non-finite values.
Results may differ from the reference program's by a relative error of at most 0.02.
Values may be sent and summed in bfloat16 or wider, within the bound.
No kernel may reach another device: no remote copies, remote signals or barrier semaphores. Data moves between devices by JAX's collectives and lax.ppermute only.
A program may use at most 64 MiB of HBM per device.

```python
import jax
import jax.numpy as jnp
from jax import lax

C = 128
C2 = 128
KVOL = 27
CHILD = 8
BLOCK = 128
NB = 16
ROWS = 2048
BRD = 256
RC = 512
N_SLAB = 4
N_TILE = 32
DEVICES = 128


def live_rows(key):
    blocks = jax.random.randint(jax.random.fold_in(key, 7), (DEVICES,), max(1, NB // 4), NB)
    return (blocks * BLOCK).astype(jnp.int32)


def draw_rulebook(key, part):
    row_count = NB * BLOCK
    empty_row = row_count + 4 * BRD
    live = live_rows(key)
    live_blocks = (live // BLOCK)[None, :, None]
    shape_blocks = (KVOL, DEVICES, NB)
    picker = jax.random.randint(jax.random.fold_in(key, 1), shape_blocks, 0, 10)
    local_block = jax.random.randint(jax.random.fold_in(key, 2), shape_blocks, 0, 1 << 20) % live_blocks
    far_block = NB + jax.random.randint(jax.random.fold_in(key, 3), shape_blocks, 0, NB // 2)
    source = jnp.where(picker < 6, local_block, far_block)
    shape = (KVOL, DEVICES, NB, BLOCK)
    inner_idx = jax.random.randint(jax.random.fold_in(key, 8), shape, 0, BLOCK)
    keeper = jax.random.randint(jax.random.fold_in(key, 9), shape, 0, 10)
    index = jnp.where(keeper < 6, source[:, :, :, None] * BLOCK + inner_idx, empty_row)
    place = jnp.arange(row_count, dtype=jnp.int32).reshape(1, 1, NB, BLOCK)
    centre = (jnp.arange(KVOL, dtype=jnp.int32) == KVOL // 2).reshape(KVOL, 1, 1, 1)
    index = jnp.where(centre, jnp.broadcast_to(place, shape), index)
    index = jnp.where(place < live.reshape(1, DEVICES, 1, 1), index, empty_row)
    return index.reshape(KVOL, DEVICES * row_count).astype(jnp.int32)


def draw_boundary_rows(key, part):
    live = live_rows(key)[:, None, None]
    picks = jax.random.randint(jax.random.fold_in(key, 6), (DEVICES, 4, BRD), 0, 1 << 20) % live
    return picks.reshape(DEVICES * 4, BRD).astype(jnp.int32)


def draw_parent_code(key, part):
    row_count = NB * BLOCK
    quarter = BLOCK // 4
    keys_all = jax.random.split(jax.random.fold_in(key, 4), DEVICES * NB)
    orders = jax.vmap(lambda key_one: jax.random.permutation(key_one, BLOCK))(keys_all).reshape(DEVICES, NB, BLOCK)
    coin = jax.random.randint(jax.random.fold_in(key, 5), (DEVICES, NB, BLOCK), 0, 2)
    inside = jnp.arange(BLOCK, dtype=jnp.int32)
    block_idx = jnp.arange(NB, dtype=jnp.int32)
    code_at = (block_idx[None, :, None] * quarter + (inside // 4)[None, None, :]) * 8 + 2 * (inside % 4)[None, None, :] + coin
    codes = jax.vmap(lambda order_one, code_one: jnp.zeros((BLOCK,), jnp.int32).at[order_one].set(code_one))(orders.reshape(DEVICES * NB, BLOCK), code_at.reshape(DEVICES * NB, BLOCK))
    codes = codes.reshape(DEVICES, row_count)
    position = jnp.arange(row_count, dtype=jnp.int32)
    live = live_rows(key)[:, None]
    codes = jnp.where(position[None, :] < live, codes, row_count // 4 * 8)
    return codes.reshape(DEVICES * row_count).astype(jnp.int32)


def block_scale(own_key, shape, cuts, smallest, high):
    def one(dim, blocks):
        heights = jax.random.uniform(jax.random.fold_in(jax.random.fold_in(own_key, 6), dim), (blocks,), jnp.float32, smallest / len(cuts), high / len(cuts))
        return jnp.repeat(jnp.exp(heights), shape[dim] // blocks).reshape((-1,) + (1,) * (len(shape) - dim - 1))

    gain = one(*cuts[0])
    for cut in cuts[1:]:
        gain = gain * one(*cut)
    return gain


def normal_values(stream_key, extent, width, bound, shards=(), kind=jnp.bfloat16):
    result = width * jax.random.normal(stream_key, extent, jnp.float32)
    if shards:
        result = result * block_scale(stream_key, extent, shards, -0.22, 0.18)
    return jnp.clip(result, -bound, bound).astype(kind)


def setup_inputs(seed: int = 0) -> dict:
    key_of = jax.random.split(jax.random.key(seed), 8)
    return {
        "features": normal_values(key_of[0], (DEVICES * ROWS, C), 1.0, 6.0, ((0, 128),)),
        "conv_weight": normal_values(key_of[1], (KVOL, C, C), (11 * C) ** -0.5, 0.15625),
        "down_weight": normal_values(key_of[2], (CHILD, C, C2), (4 * C) ** -0.5, 0.25),
        "coarse_grad": normal_values(key_of[3], (DEVICES * RC, C2), 1.0, 6.0, ((0, 128),)),
        "rulebook": draw_rulebook(jax.random.fold_in(key_of[7], 71), 0),
        "boundary_rows": draw_boundary_rows(jax.random.fold_in(key_of[7], 71), 0),
        "parent_code": draw_parent_code(jax.random.fold_in(key_of[7], 71), 0),
    }


def reference(features, conv_weight, down_weight, coarse_grad, rulebook, boundary_rows, parent_code):
    part_count = N_SLAB * N_TILE
    row_count = NB * BLOCK
    coarse_rows = row_count // 4
    empty_row = row_count + 4 * BRD
    feat_all = features.reshape(part_count, row_count, C)
    lists_all = boundary_rows.reshape(part_count, 4, BRD)
    sent_all = jax.vmap(lambda feat_one, list_one: feat_one[list_one])(feat_all, lists_all)
    sent_grid = sent_all.reshape(N_SLAB, N_TILE, 4, BRD, C)
    zero_slab = jnp.zeros((1, N_TILE, BRD, C), jnp.bfloat16)
    zero_tile = jnp.zeros((N_SLAB, 1, BRD, C), jnp.bfloat16)
    from_below = jnp.concatenate([zero_slab, sent_grid[:-1, :, 0]], axis=0)
    from_above = jnp.concatenate([sent_grid[1:, :, 1], zero_slab], axis=0)
    from_left = jnp.concatenate([zero_tile, sent_grid[:, :-1, 2]], axis=1)
    from_right = jnp.concatenate([sent_grid[:, 1:, 3], zero_tile], axis=1)
    received = jnp.stack([from_below, from_above, from_left, from_right], axis=2)
    received = received.reshape(part_count, 4 * BRD, C)
    book_all = rulebook.reshape(KVOL, part_count, row_count).transpose(1, 0, 2)
    code_all = parent_code.reshape(part_count, row_count)
    grad_all = coarse_grad.reshape(part_count, coarse_rows, C2)
    down_flat = down_weight.astype(jnp.float32).reshape(CHILD * C, C2)
    conv_float = conv_weight.astype(jnp.float32)

    def one_part(totals, item):
        feat_one, recv_one, book_one, code_one, grad_one = item
        extended = jnp.concatenate([feat_one, recv_one, jnp.zeros((1, C), jnp.bfloat16)], axis=0)
        gathered = extended[book_one].astype(jnp.float32)
        pre = jnp.einsum('krc,kcd->rd', gathered, conv_float)
        hidden = jnp.maximum(pre, 0.0).astype(jnp.bfloat16)
        parent = code_one // 8
        slot_idx = code_one % 8
        has_parent = parent < coarse_rows
        onehot = (slot_idx[:, None] == jnp.arange(CHILD, dtype=jnp.int32)[None, :]) & has_parent[:, None]
        spread = (hidden.astype(jnp.float32)[:, None, :] * onehot[:, :, None].astype(jnp.float32)).reshape(row_count, CHILD * C)
        terms = jnp.dot(spread, down_flat)
        coarse_one = jnp.zeros((coarse_rows + 1, C2), jnp.float32).at[parent].add(terms)[:coarse_rows]
        grad_ext = jnp.concatenate([grad_one, jnp.zeros((1, C2), jnp.bfloat16)], axis=0)
        grad_rows = grad_ext[parent].astype(jnp.float32)
        spread_grad = jnp.dot(grad_rows, down_flat.T).reshape(row_count, CHILD, C)
        hidden_grad = jnp.sum(spread_grad * onehot[:, :, None].astype(jnp.float32), axis=1)
        pre_grad = jnp.where(pre > 0, hidden_grad, 0.0).astype(jnp.bfloat16).astype(jnp.float32)
        down_part = jnp.dot(spread.T, grad_rows)
        conv_part = jnp.einsum('krc,rd->kcd', gathered, pre_grad)
        back = jnp.einsum('rd,kcd->krc', pre_grad, conv_float)
        ext_grad = jnp.zeros((empty_row + 1, C), jnp.float32).at[book_one].add(back)
        new_totals = (totals[0] + conv_part, totals[1] + down_part)
        return new_totals, (coarse_one.astype(jnp.bfloat16), ext_grad[:row_count], ext_grad[row_count:empty_row])

    start = (jnp.zeros((KVOL, C, C), jnp.float32), jnp.zeros((CHILD * C, C2), jnp.float32))
    totals, stacked = lax.scan(one_part, start, (feat_all, received, book_all, code_all, grad_all))
    coarse_all, local_grad, halo_grad = stacked
    halo_grid = halo_grad.reshape(N_SLAB, N_TILE, 4, BRD, C)
    zero_slab_f = jnp.zeros((1, N_TILE, BRD, C), jnp.float32)
    zero_tile_f = jnp.zeros((N_SLAB, 1, BRD, C), jnp.float32)
    back_zero = jnp.concatenate([halo_grid[1:, :, 0], zero_slab_f], axis=0)
    back_one = jnp.concatenate([zero_slab_f, halo_grid[:-1, :, 1]], axis=0)
    back_two = jnp.concatenate([halo_grid[:, 1:, 2], zero_tile_f], axis=1)
    back_three = jnp.concatenate([zero_tile_f, halo_grid[:, :-1, 3]], axis=1)
    returned = jnp.stack([back_zero, back_one, back_two, back_three], axis=2).reshape(part_count, 4 * BRD, C)
    input_grad = jax.vmap(lambda grad_one, list_one, ret_one: grad_one.at[list_one].add(ret_one))(local_grad, lists_all.reshape(part_count, 4 * BRD), returned)
    return (coarse_all.reshape(part_count * coarse_rows, C2), input_grad.reshape(part_count * row_count, C), totals[0], totals[1].reshape(CHILD, C, C2))
```

```python
import functools

import jax
import jax.numpy as jnp
from jax import lax
from jax.experimental import pallas as pl
from jax.experimental.pallas import tpu as pltpu
from jax.sharding import PartitionSpec as P

BLOCK = 128
BF = jnp.bfloat16
F32 = jnp.float32
VMEM_LIMIT = 56 * 1024 * 1024
VM = pl.BlockSpec(memory_space=pltpu.VMEM)
SM = pl.BlockSpec(memory_space=pltpu.SMEM)

NN = (((1,), (0,)), ((), ()))
NT = (((1,), (1,)), ((), ()))
TN = (((0,), (0,)), ((), ()))


def mm(a, b, dims=NN):
    return lax.dot_general(a, b, dims, preferred_element_type=F32)


def sub_iota(rows, dtype=F32):
    return lax.broadcasted_iota(jnp.int32, (rows, BLOCK), 0).astype(F32).astype(dtype)


def onehot_t(row, ids):
    wide = jnp.broadcast_to(row, (16, BLOCK)).astype(BF)
    wide = jnp.concatenate([wide] * (ids.shape[0] // 16), axis=0)
    return jnp.where(ids == wide, jnp.ones((), BF), jnp.zeros((), BF))


def pick_kernel(feat_ref, rows_ref, out_ref, xt_ref):
    blocks = feat_ref.shape[0] // BLOCK
    for b in range(blocks):
        xt_ref[b] = feat_ref[b * BLOCK : (b + 1) * BLOCK, :].T
    ids = sub_iota(BLOCK, jnp.int32)
    for g in range(rows_ref.shape[0]):
        row = rows_ref[g : g + 1, :]
        acc = jnp.zeros((BLOCK, BLOCK), F32)
        for b in range(blocks):
            hot = onehot_i(row - b * BLOCK, ids)
            acc = acc + mm(xt_ref[b], hot)
        out_ref[g * BLOCK : (g + 1) * BLOCK, :] = acc.T.astype(BF)


def onehot_i(row, ids):
    return jnp.where(ids == row, 1.0, 0.0).astype(BF)


def main_kernel(
    src_ref, xt_loc_ref, recv_ref, book_ref, cell_ref, w_ref, dw_ref, cg_ref,
    coarse_ref, pgt_ref, part_ref,
    xt_ref, wt_ref, gt_ref, conv_ref, sg_ref, ch_ref,
):
    kvol = w_ref.shape[0]
    blocks = xt_loc_ref.shape[0]
    far = recv_ref.shape[0] // BLOCK
    child = dw_ref.shape[0]
    quarter = cg_ref.shape[0] // blocks
    ids = sub_iota(BLOCK, BF)
    ids2 = jnp.concatenate([ids, ids + jnp.asarray(BLOCK, BF)], axis=0)

    for k in range(kvol):
        wt_ref[:, k * BLOCK : (k + 1) * BLOCK] = w_ref[k].T
    for b in range(blocks):
        xt_ref[b] = xt_loc_ref[b]
    for b in range(far):
        xt_ref[blocks + b] = recv_ref[b * BLOCK : (b + 1) * BLOCK, :].T
    xt_ref[blocks + far] = jnp.zeros((BLOCK, BLOCK), BF)
    for j in range(child):
        part = mm(cg_ref[...], dw_ref[j], NT).astype(BF)
        for b in range(blocks):
            sg_ref[b, j * quarter : (j + 1) * quarter, :] = part[b * quarter : (b + 1) * quarter, :]
    conv_ref[...] = jnp.zeros_like(conv_ref)

    @pl.loop(0, blocks // 2)
    def _(p):
        for k in range(kvol):
            for h in range(2):
                b = 2 * p + h
                hot = onehot_t(book_ref[k, pl.ds(b, 1), :], ids)
                got = mm(xt_ref[src_ref[k, b]], hot)
                gt_ref[k * BLOCK : (k + 1) * BLOCK, h * BLOCK : (h + 1) * BLOCK] = got.astype(BF)
        pre = mm(wt_ref[...], gt_ref[...])
        hid = jnp.maximum(pre, 0.0).astype(BF)
        halves = []
        for h in range(2):
            b = 2 * p + h
            hot = onehot_t(cell_ref[pl.ds(b, 1), :], ids2)
            kids = mm(hot, hid[:, h * BLOCK : (h + 1) * BLOCK], NT).astype(BF)
            for j in range(child):
                ch_ref[pl.ds(pl.multiple_of(b * quarter, quarter), quarter), j * BLOCK : (j + 1) * BLOCK] = (
                    kids[j * quarter : (j + 1) * quarter, :]
                )
            halves.append(mm(sg_ref[b], hot, TN))
        grad = jnp.concatenate(halves, axis=1)
        pgt = jnp.where(pre > 0, grad, 0.0).astype(BF)
        pgt_ref[p] = pgt
        conv_ref[...] += mm(gt_ref[...], pgt, NT)

    kids = ch_ref[...]
    coarse_ref[...] = mm(kids, dw_ref[...].reshape(child * BLOCK, BLOCK)).astype(BF)
    rows = kvol * BLOCK
    part_ref[0:rows, :] = conv_ref[...].astype(BF)
    part_ref[rows : rows + child * BLOCK, :] = mm(kids, cg_ref[...], TN).astype(BF)
    rest = part_ref.shape[0] - rows - child * BLOCK
    part_ref[rows + child * BLOCK :, :] = jnp.zeros((rest, BLOCK), BF)


def back_kernel(src_ref, book_ref, w_ref, pgt_ref, local_ref, far_ref, acc_ref):
    kvol = w_ref.shape[0]
    blocks = local_ref.shape[0] // BLOCK
    far = far_ref.shape[0] // BLOCK
    ids = sub_iota(BLOCK, BF)
    acc_ref[...] = jnp.zeros_like(acc_ref)

    @pl.loop(0, blocks // 2)
    def _(p):
        pgt = pgt_ref[p]
        for k in range(kvol):
            back = mm(w_ref[k], pgt).astype(BF)
            for h in range(2):
                b = 2 * p + h
                hot = onehot_t(book_ref[k, pl.ds(b, 1), :], ids)
                acc_ref[h, src_ref[k, b]] += mm(hot, back[:, h * BLOCK : (h + 1) * BLOCK], NT)

    for b in range(blocks):
        local_ref[b * BLOCK : (b + 1) * BLOCK, :] = acc_ref[0, b] + acc_ref[1, b]
    for b in range(far):
        far_ref[b * BLOCK : (b + 1) * BLOCK, :] = (acc_ref[0, blocks + b] + acc_ref[1, blocks + b]).astype(BF)


def add_kernel(local_ref, rows_ref, ret_ref, out_ref):
    blocks = local_ref.shape[0] // BLOCK
    groups = rows_ref.shape[0]
    ids = sub_iota(BLOCK, jnp.int32)
    for b in range(blocks):
        hot = jnp.concatenate([onehot_i(rows_ref[g : g + 1, :] - b * BLOCK, ids) for g in range(groups)], axis=1)
        out_ref[b * BLOCK : (b + 1) * BLOCK, :] = local_ref[b * BLOCK : (b + 1) * BLOCK, :] + mm(hot, ret_ref[...])


def call(kernel, outs, ins, scratch=()):
    single = len(outs) == 1
    shapes = tuple(jax.ShapeDtypeStruct(s, d) for s, d in outs)
    return pl.pallas_call(
        kernel,
        out_shape=shapes[0] if single else shapes,
        in_specs=ins,
        out_specs=VM if single else tuple(VM for _ in outs),
        scratch_shapes=list(scratch),
        compiler_params=pltpu.CompilerParams(vmem_limit_bytes=VMEM_LIMIT),
    )


def wide(v):
    return v.astype(F32)


def total_over_devices(y):
    tile, slab = lax.axis_index("tile"), lax.axis_index("slab")
    chips = lax.axis_size("tile") // 8
    index = {"c": tile % 2, "z": (tile // 2) % 4, "y": tile // 8, "x": slab}
    stride = {"c": 1, "z": 2, "y": 8}
    size = {"c": 2, "z": 4, "y": chips}

    def send(v, axis, to):
        if axis == "x":
            return lax.ppermute(v, "slab", [(i, to(i)) for i in range(lax.axis_size("slab"))])
        st, n = stride[axis], size[axis]
        pairs = []
        for i in range(lax.axis_size("tile")):
            q = (i // st) % n
            pairs.append((i, i + (to(q) - q) * st))
        return lax.ppermute(v, "tile", pairs)

    def split4(v, axis):
        i, m = index[axis], v.shape[0] // 4
        total = wide(lax.dynamic_slice_in_dim(v, i * m, m, 0))
        got = []
        for sh in (2, 1, 3):
            piece = lax.dynamic_slice_in_dim(v, ((i + sh) % 4) * m, m, 0)
            got.append(send(piece, axis, lambda q, sh=sh: (q + sh) % 4))
        for g in got:
            total = total + wide(g)
        return total.astype(BF)

    def join4(v, axis):
        i, m = index[axis], v.shape[0]
        out = jnp.zeros((4 * m, v.shape[1]), v.dtype)
        out = lax.dynamic_update_slice_in_dim(out, v, i * m, 0)
        got = [(sh, send(v, axis, lambda q, sh=sh: (q + sh) % 4)) for sh in (2, 1, 3)]
        for sh, g in got:
            out = lax.dynamic_update_slice_in_dim(out, g, ((i - sh) % 4) * m, 0)
        return out

    def all4(v, axis):
        g = {sh: wide(send(v, axis, lambda q, sh=sh: (q + sh) % 4)) for sh in (2, 1, 3)}
        return ((wide(v) + g[2]) + (g[1] + g[3])).astype(BF)

    half = y.shape[0] // 2
    core = index["c"]
    keep = lax.dynamic_slice_in_dim(y, core * half, half, 0)
    give = lax.dynamic_slice_in_dim(y, (1 - core) * half, half, 0)
    y = (wide(keep) + wide(send(give, "c", lambda q: 1 - q))).astype(BF)
    y = split4(y, "x")
    y = split4(y, "y")
    y = all4(y, "z")
    y = join4(y, "y")
    y = join4(y, "x")
    other = send(y, "c", lambda q: 1 - q)
    first = jnp.where(core == 0, y, other)
    second = jnp.where(core == 0, other, y)
    return jnp.concatenate([first, second], axis=0)


def body(features, conv_weight, down_weight, coarse_grad, rulebook, boundary_rows, parent_code):
    row_count, chans = features.shape
    coarse_rows, out_chans = coarse_grad.shape
    list_len = boundary_rows.shape[1]
    child = down_weight.shape[0]
    kvol = conv_weight.shape[0]
    blocks = row_count // BLOCK
    far_rows = 4 * list_len
    quarter = coarse_rows // blocks
    slabs, tiles = lax.axis_size("slab"), lax.axis_size("tile")

    lists = boundary_rows.reshape(far_rows // BLOCK, BLOCK)
    outgoing, xt = call(
        pick_kernel, [((far_rows, chans), BF), ((blocks, BLOCK, BLOCK), BF)], [VM, VM]
    )(features, lists)
    outgoing = outgoing.reshape(4, list_len, chans)
    up = {"slab": [(i, i + 1) for i in range(slabs - 1)], "tile": [(i, i + 1) for i in range(tiles - 1)]}
    down = {a: [(j, i) for i, j in pairs] for a, pairs in up.items()}
    received = jnp.concatenate(
        [
            lax.ppermute(outgoing[0], "slab", up["slab"]),
            lax.ppermute(outgoing[1], "slab", down["slab"]),
            lax.ppermute(outgoing[2], "tile", up["tile"]),
            lax.ppermute(outgoing[3], "tile", down["tile"]),
        ]
    )

    book = rulebook.reshape(kvol, blocks, BLOCK)
    source = jnp.min(book, axis=2) // BLOCK
    inner = (book - source[:, :, None] * BLOCK).astype(F32)
    code = parent_code.reshape(blocks, BLOCK)
    cell = (code % child) * quarter + code // child - jnp.arange(blocks, dtype=jnp.int32)[:, None] * quarter
    cell = jnp.where(code < child * coarse_rows, cell, -1).astype(F32)

    grad_rows = (kvol + child) * BLOCK
    part_rows = -(-grad_rows // 512) * 512
    table = blocks + far_rows // BLOCK + 1
    coarse, pgt, part = call(
        main_kernel,
        [((coarse_rows, out_chans), BF), ((blocks // 2, BLOCK, 2 * BLOCK), BF), ((part_rows, out_chans), BF)],
        [SM] + [VM] * 7,
        [
            pltpu.VMEM((table, BLOCK, BLOCK), BF),
            pltpu.VMEM((BLOCK, kvol * BLOCK), BF),
            pltpu.VMEM((kvol * BLOCK, 2 * BLOCK), BF),
            pltpu.VMEM((kvol * BLOCK, BLOCK), F32),
            pltpu.VMEM((blocks, child * quarter, BLOCK), BF),
            pltpu.VMEM((coarse_rows, child * BLOCK), BF),
        ],
    )(source, xt, received, inner, cell, conv_weight, down_weight, coarse_grad)

    total = total_over_devices(part)

    local, far = call(
        back_kernel,
        [((row_count, chans), F32), ((far_rows, chans), BF)],
        [SM] + [VM] * 3,
        [pltpu.VMEM((2, table, BLOCK, BLOCK), F32)],
    )(source, inner, conv_weight, pgt)
    far = far.reshape(4, list_len, chans)
    returned = jnp.concatenate(
        [
            lax.ppermute(far[0], "slab", down["slab"]),
            lax.ppermute(far[1], "slab", up["slab"]),
            lax.ppermute(far[2], "tile", down["tile"]),
            lax.ppermute(far[3], "tile", up["tile"]),
        ]
    )
    input_grad = call(add_kernel, [((row_count, chans), F32)], [VM] * 3)(local, lists, returned)
    total = total.astype(F32)
    return (
        coarse,
        input_grad,
        total[: kvol * BLOCK].reshape(kvol, chans, chans),
        total[kvol * BLOCK : grad_rows].reshape(child, chans, out_chans),
    )


def solution(mesh):
    return jax.shard_map(
        body,
        mesh=mesh,
        in_specs=(
            P(("slab", "tile"), None),
            P(),
            P(),
            P(("slab", "tile"), None),
            P(None, ("slab", "tile")),
            P(("slab", "tile"), None),
            P(("slab", "tile")),
        ),
        out_specs=(P(("slab", "tile"), None), P(("slab", "tile"), None), P(), P()),
        check_vma=False,
    )
```

```python
import functools

import jax
import jax.numpy as jnp
from jax import lax
from jax.experimental import pallas as pl
from jax.experimental.pallas import tpu as pltpu
from jax.sharding import PartitionSpec as P

BLOCK = 128
BF = jnp.bfloat16
F32 = jnp.float32
VMEM_LIMIT = 56 * 1024 * 1024
VM = pl.BlockSpec(memory_space=pltpu.VMEM)
SM = pl.BlockSpec(memory_space=pltpu.SMEM)

NN = (((1,), (0,)), ((), ()))
NT = (((1,), (1,)), ((), ()))
TN = (((0,), (0,)), ((), ()))


def mm(a, b, dims=NN):
    return lax.dot_general(a, b, dims, preferred_element_type=F32)


def sub_iota(rows, dtype=F32):
    return lax.broadcasted_iota(jnp.int32, (rows, BLOCK), 0).astype(F32).astype(dtype)


def onehot_t(row, ids):
    wide = jnp.broadcast_to(row, (16, BLOCK)).astype(BF)
    wide = jnp.concatenate([wide] * (ids.shape[0] // 16), axis=0)
    return jnp.where(ids == wide, jnp.ones((), BF), jnp.zeros((), BF))


def pick_kernel(feat_ref, rows_ref, *refs):
    out_refs, xt_ref, full_ref, hot_ref = refs[:-3], refs[-3], refs[-2], refs[-1]
    blocks = feat_ref.shape[0] // BLOCK
    length = rows_ref.shape[1]
    for b in range(blocks):
        block = feat_ref[b * BLOCK : (b + 1) * BLOCK, :].T
        xt_ref[b] = block
        full_ref[:, b * BLOCK : (b + 1) * BLOCK] = block
    ids = sub_iota(BLOCK, BF)
    for d, out_ref in enumerate(out_refs):
        for g in range(length // BLOCK):
            row = rows_ref[d : d + 1, g * BLOCK : (g + 1) * BLOCK]
            for b in range(blocks):
                hot_ref[b * BLOCK : (b + 1) * BLOCK, g * BLOCK : (g + 1) * BLOCK] = onehot_t(
                    (row - b * BLOCK).astype(F32), ids
                )
        out_ref[...] = mm(full_ref[...], hot_ref[...]).T.astype(BF)


def main_kernel(
    src_ref, core_ref, xt_loc_ref, r0_ref, r1_ref, r2_ref, r3_ref, book_ref, cell_ref, w_ref, dw_ref, cg_ref,
    coarse_ref, pg_ref, wt_ref, keep_ref, give_ref,
    xt_ref, gt_ref, conv_ref, sg_ref, ch_ref, part_ref,
):
    kvol = w_ref.shape[0]
    blocks = xt_loc_ref.shape[0]
    recv_refs = (r0_ref, r1_ref, r2_ref, r3_ref)
    each = r0_ref.shape[0] // BLOCK
    far = 4 * each
    child = dw_ref.shape[0]
    quarter = cg_ref.shape[0] // blocks
    ids = sub_iota(BLOCK, BF)
    ids2 = jnp.concatenate([ids, ids + jnp.asarray(BLOCK, BF)], axis=0)

    for k in range(kvol):
        wt_ref[:, k * BLOCK : (k + 1) * BLOCK] = w_ref[k].T
    for b in range(blocks):
        xt_ref[b] = xt_loc_ref[b]
    for b in range(far):
        one = b % each
        xt_ref[blocks + b] = recv_refs[b // each][one * BLOCK : (one + 1) * BLOCK, :].T
    xt_ref[blocks + far] = jnp.zeros((BLOCK, BLOCK), BF)
    for j in range(child):
        part = mm(cg_ref[...], dw_ref[j], NT).astype(BF)
        for b in range(blocks):
            sg_ref[b, j * quarter : (j + 1) * quarter, :] = part[b * quarter : (b + 1) * quarter, :]
    conv_ref[...] = jnp.zeros_like(conv_ref)

    @pl.loop(0, blocks // 2)
    def _(p):
        for k in range(kvol):
            for h in range(2):
                b = 2 * p + h
                hot = onehot_t(book_ref[k, pl.ds(b, 1), :], ids)
                got = mm(xt_ref[src_ref[k, b]], hot)
                gt_ref[k * BLOCK : (k + 1) * BLOCK, h * BLOCK : (h + 1) * BLOCK] = got.astype(BF)
        pre = mm(wt_ref[...], gt_ref[...])
        hid = jnp.maximum(pre, 0.0).astype(BF)
        halves = []
        for h in range(2):
            b = 2 * p + h
            hot = onehot_t(cell_ref[pl.ds(b, 1), :], ids2)
            kids = mm(hot, hid[:, h * BLOCK : (h + 1) * BLOCK], NT).astype(BF)
            for j in range(child):
                ch_ref[pl.ds(pl.multiple_of(b * quarter, quarter), quarter), j * BLOCK : (j + 1) * BLOCK] = (
                    kids[j * quarter : (j + 1) * quarter, :]
                )
            halves.append(mm(sg_ref[b], hot, TN))
        grad = jnp.concatenate(halves, axis=1)
        pgt = jnp.where(pre > 0, grad, 0.0).astype(BF)
        pg = pgt.T
        pg_ref[p] = pg
        conv_ref[...] += mm(gt_ref[...], pg)

    kids = ch_ref[...]
    coarse_ref[...] = mm(kids, dw_ref[...].reshape(child * BLOCK, BLOCK)).astype(BF)
    rows = kvol * BLOCK
    part_ref[0:rows, :] = conv_ref[...].astype(BF)
    part_ref[rows : rows + child * BLOCK, :] = mm(kids, cg_ref[...], TN).astype(BF)
    rest = part_ref.shape[0] - rows - child * BLOCK
    part_ref[rows + child * BLOCK :, :] = jnp.zeros((rest, BLOCK), BF)
    half = keep_ref.shape[0]
    core = core_ref[0]
    keep_ref[...] = part_ref[pl.ds(pl.multiple_of(core * half, half), half), :]
    give_ref[...] = part_ref[pl.ds(pl.multiple_of((1 - core) * half, half), half), :]


def back_kernel(lo, hi, src_ref, book_ref, wt_ref, pg_ref, *refs):
    if lo == 0:
        table_ref, back_ref = refs
        table_ref[...] = jnp.zeros_like(table_ref)
    else:
        before_ref, table_ref, back_ref = refs
        table_ref[...] = before_ref[...]
    kvol = book_ref.shape[0]
    ids = sub_iota(BLOCK, BF)

    @pl.loop(lo, hi)
    def _(p):
        back_ref[...] = mm(pg_ref[p], wt_ref[...]).astype(BF)
        for k in range(kvol):
            for h in range(2):
                b = 2 * p + h
                hot = onehot_t(book_ref[k, pl.ds(b, 1), :], ids)
                table_ref[src_ref[k, b]] += mm(
                    hot, back_ref[h * BLOCK : (h + 1) * BLOCK, k * BLOCK : (k + 1) * BLOCK]
                )


def add_kernel(table_ref, rows_ref, g0_ref, g1_ref, g2_ref, g3_ref, out_ref, ret_ref):
    blocks = out_ref.shape[0] // BLOCK
    lists, length = rows_ref.shape
    ids = sub_iota(BLOCK, BF)
    for d, got_ref in enumerate((g0_ref, g1_ref, g2_ref, g3_ref)):
        ret_ref[d * length : (d + 1) * length, :] = got_ref[...]
    groups = [
        rows_ref[d : d + 1, g * BLOCK : (g + 1) * BLOCK] for d in range(lists) for g in range(length // BLOCK)
    ]
    for b in range(blocks):
        hot = jnp.concatenate([onehot_t((row - b * BLOCK).astype(F32), ids) for row in groups], axis=1)
        out_ref[b * BLOCK : (b + 1) * BLOCK, :] = table_ref[b] + mm(hot, ret_ref[...])


def spread_kernel(core_ref, own_ref, other_ref, conv_ref, down_ref):
    half = own_ref.shape[0]
    rows = conv_ref.shape[0]

    def put(low_ref, high_ref):
        conv_ref[0:half, :] = low_ref[...].astype(F32)
        conv_ref[half:rows, :] = high_ref[0 : rows - half, :].astype(F32)
        down_ref[...] = high_ref[rows - half : rows - half + down_ref.shape[0], :].astype(F32)

    @pl.when(core_ref[0] == 0)
    def _():
        put(own_ref, other_ref)

    @pl.when(core_ref[0] != 0)
    def _():
        put(other_ref, own_ref)


def call(kernel, outs, ins, scratch=(), aliases=None):
    single = len(outs) == 1
    shapes = tuple(jax.ShapeDtypeStruct(s, d) for s, d in outs)
    return pl.pallas_call(
        kernel,
        out_shape=shapes[0] if single else shapes,
        in_specs=ins,
        out_specs=VM if single else tuple(VM for _ in outs),
        scratch_shapes=list(scratch),
        input_output_aliases=aliases or {},
        compiler_params=pltpu.CompilerParams(vmem_limit_bytes=VMEM_LIMIT),
    )


def wide(v):
    return v.astype(F32)


def tie(*values):
    return lax.optimization_barrier(values)


def body(features, conv_weight, down_weight, coarse_grad, rulebook, boundary_rows, parent_code):
    row_count, chans = features.shape
    coarse_rows, out_chans = coarse_grad.shape
    list_len = boundary_rows.shape[1]
    child = down_weight.shape[0]
    kvol = conv_weight.shape[0]
    blocks = row_count // BLOCK
    pairs = blocks // 2
    far_rows = 4 * list_len
    quarter = coarse_rows // blocks
    slabs, tiles = lax.axis_size("slab"), lax.axis_size("tile")
    place = lax.axis_index("slab") * tiles + lax.axis_index("tile")
    core = place & 1

    *outgoing, xt = call(
        pick_kernel,
        [((list_len, chans), BF)] * 4 + [((blocks, BLOCK, BLOCK), BF)],
        [VM, VM],
        [pltpu.VMEM((BLOCK, row_count), BF), pltpu.VMEM((row_count, list_len), BF)],
    )(features, boundary_rows)
    up = {"slab": [(i, i + 1) for i in range(slabs - 1)], "tile": [(i, i + 1) for i in range(tiles - 1)]}
    down = {a: [(j, i) for i, j in links] for a, links in up.items()}
    received = [
        lax.ppermute(outgoing[0], "slab", up["slab"]),
        lax.ppermute(outgoing[1], "slab", down["slab"]),
        lax.ppermute(outgoing[2], "tile", up["tile"]),
        lax.ppermute(outgoing[3], "tile", down["tile"]),
    ]

    book = rulebook.reshape(kvol, blocks, BLOCK)
    source = jnp.min(book, axis=2) // BLOCK
    inner = (book - source[:, :, None] * BLOCK).astype(F32)
    code = parent_code.reshape(blocks, BLOCK)
    cell = (code % child) * quarter + code // child - jnp.arange(blocks, dtype=jnp.int32)[:, None] * quarter
    cell = jnp.where(code < child * coarse_rows, cell, -1).astype(F32)

    grad_rows = (kvol + child) * BLOCK
    part_rows = -(-grad_rows // 512) * 512
    table = blocks + far_rows // BLOCK + 1
    core_one = core.reshape(1)
    coarse, pg, wt, keep, give = call(
        main_kernel,
        [
            ((coarse_rows, out_chans), BF),
            ((pairs, 2 * BLOCK, BLOCK), BF),
            ((BLOCK, kvol * BLOCK), BF),
            ((part_rows // 2, out_chans), BF),
            ((part_rows // 2, out_chans), BF),
        ],
        [SM, SM] + [VM] * 10,
        [
            pltpu.VMEM((table, BLOCK, BLOCK), BF),
            pltpu.VMEM((kvol * BLOCK, 2 * BLOCK), BF),
            pltpu.VMEM((kvol * BLOCK, BLOCK), F32),
            pltpu.VMEM((blocks, child * quarter, BLOCK), BF),
            pltpu.VMEM((coarse_rows, child * BLOCK), BF),
            pltpu.VMEM((part_rows, BLOCK), BF),
        ],
    )(source, core_one, xt, *received, inner, cell, conv_weight, down_weight, coarse_grad)

    def back_part(acc, lo, hi):
        ins = (source, inner, wt, pg) + (() if acc is None else (acc,))
        return call(
            functools.partial(back_kernel, lo, hi),
            [((table, BLOCK, BLOCK), F32)],
            [SM] + [VM] * (len(ins) - 1),
            [pltpu.VMEM((2 * BLOCK, kvol * BLOCK), BF)],
            aliases={} if acc is None else {4: 0},
        )(*ins)

    stride = {"c": 1, "z": 2, "y": 8, "x": tiles}
    size = {"c": 2, "z": 4, "y": tiles // 8, "x": slabs}

    def send(v, axes, to):
        links = []
        for i in range(slabs * tiles):
            axis = axes[i % 2]
            st, n = stride[axis], size[axis]
            q = (i // st) % n
            links.append((i, i + (to(q) % n - q) * st))
        return lax.ppermute(v, ("slab", "tile"), links)

    def spot(axes):
        first, second = [(place >> (stride[a].bit_length() - 1)) & (size[a] - 1) for a in axes]
        return jnp.where(core == 0, first, second)

    def shifts(axes, pieces):
        return [send(v, axes, lambda q, sh=sh: q + sh) for sh, v in zip((1, 2, 3), pieces)]

    order = ("xy", "yz", "zx", "xy")
    swap = send(give, "cc", lambda q: 1 - q)
    acc = back_part(None, 0, 2)
    swap, acc = tie(swap, acc)
    y = (wide(keep) + wide(swap)).astype(BF)

    i, m = spot(order[0]), y.shape[0] // 4
    mine = lax.dynamic_slice_in_dim(y, i * m, m, 0)
    got = shifts(order[0], [lax.dynamic_slice_in_dim(y, ((i + sh) & 3) * m, m, 0) for sh in (1, 2, 3)])
    acc = back_part(acc, 2, 4)
    *got, acc = tie(*got, acc)
    y = ((wide(mine) + wide(got[1])) + (wide(got[0]) + wide(got[2]))).astype(BF)

    for ph, (lo, hi) in ((1, (4, 6)), (2, (6, 8))):
        y, acc = tie(y, acc)
        got = shifts(order[ph], [y] * 3)
        acc = back_part(acc, lo, hi)
        *got, acc = tie(*got, acc)
        y = ((wide(y) + wide(got[1])) + (wide(got[0]) + wide(got[2]))).astype(BF)

    y, acc = tie(y, acc)
    i = spot(order[3])
    got = shifts(order[3], [y] * 3)
    far = acc[blocks : table - 1].astype(BF).reshape(4, list_len, chans)
    returned = [
        lax.ppermute(far[0], "slab", down["slab"]),
        lax.ppermute(far[1], "slab", up["slab"]),
        lax.ppermute(far[2], "tile", down["tile"]),
        lax.ppermute(far[3], "tile", up["tile"]),
    ]
    full = jnp.zeros((4 * m, out_chans), BF)
    for sh, v in zip((0, 1, 2, 3), [y] + got):
        full = lax.dynamic_update_slice_in_dim(full, v, ((i + 4 - sh) & 3) * m, 0)
    other = send(full, "cc", lambda q: 1 - q)
    input_grad = call(
        add_kernel, [((row_count, chans), F32)], [VM] * 6, [pltpu.VMEM((far_rows, chans), BF)]
    )(acc, boundary_rows, *returned)
    conv_grad, down_grad = call(
        spread_kernel,
        [((kvol * BLOCK, out_chans), F32), ((child * BLOCK, out_chans), F32)],
        [SM, VM, VM],
    )(core_one, full, other)
    return (
        coarse,
        input_grad,
        conv_grad.reshape(kvol, chans, chans),
        down_grad.reshape(child, chans, out_chans),
    )


def solution(mesh):
    return jax.shard_map(
        body,
        mesh=mesh,
        in_specs=(
            P(("slab", "tile"), None),
            P(),
            P(),
            P(("slab", "tile"), None),
            P(None, ("slab", "tile")),
            P(("slab", "tile"), None),
            P(("slab", "tile")),
        ),
        out_specs=(P(("slab", "tile"), None), P(("slab", "tile"), None), P(), P()),
        check_vma=False,
    )
```

```python
import functools

import jax
import jax.numpy as jnp
from jax import lax
from jax.experimental import pallas as pl
from jax.experimental.pallas import tpu as pltpu
from jax.sharding import PartitionSpec as P

BLOCK = 128
BF = jnp.bfloat16
F32 = jnp.float32
VMEM_LIMIT = 56 * 1024 * 1024
VM = pl.BlockSpec(memory_space=pltpu.VMEM)
SM = pl.BlockSpec(memory_space=pltpu.SMEM)

NN = (((1,), (0,)), ((), ()))
NT = (((1,), (1,)), ((), ()))
TN = (((0,), (0,)), ((), ()))


def mm(a, b, dims=NN):
    return lax.dot_general(a, b, dims, preferred_element_type=F32)


def sub_iota(rows, dtype=F32):
    return lax.broadcasted_iota(jnp.int32, (rows, BLOCK), 0).astype(F32).astype(dtype)


def onehot_t(row, ids):
    wide = jnp.broadcast_to(row, (16, BLOCK)).astype(BF)
    wide = jnp.concatenate([wide] * (ids.shape[0] // 16), axis=0)
    return jnp.where(ids == wide, jnp.ones((), BF), jnp.zeros((), BF))


def list_order(core, rows_ref):
    rows = [rows_ref[d : d + 1, :] for d in range(4)]
    return (rows[0], rows[1], jnp.where(core == 0, rows[2], rows[3]), jnp.where(core == 0, rows[3], rows[2]))


def slot_order(core):
    return (0, 1, 3 - core, 2 + core)


def index_kernel(book_ref, code_ref, src_ref, inner_ref, cell_ref):
    kvol = book_ref.shape[0]
    blocks, child, quarter = cell_ref.shape[0], 8, BLOCK // 4
    lane = lax.broadcasted_iota(jnp.int32, (kvol, BLOCK), 1)
    found = jnp.zeros((kvol, BLOCK), jnp.int32)
    for b in range(blocks):
        book = book_ref[:, b * BLOCK : (b + 1) * BLOCK]
        block = jnp.min(book, axis=1, keepdims=True) // BLOCK
        inner_ref[b] = (book - block * BLOCK).astype(F32)
        found = jnp.where(lane == b, block, found)
        code = code_ref[:, b * BLOCK : (b + 1) * BLOCK]
        cell = (code % child) * quarter + code // child - b * quarter
        cell_ref[b : b + 1, :] = jnp.where(code < child * quarter * blocks, cell, -1).astype(F32)
    src_ref[...] = found


def pick_kernel(core_ref, feat_ref, rows_ref, *refs):
    out_refs, xt_ref, full_ref, hot_ref = refs[:-3], refs[-3], refs[-2], refs[-1]
    blocks = feat_ref.shape[0] // BLOCK
    length = rows_ref.shape[1]
    for b in range(blocks):
        block = feat_ref[b * BLOCK : (b + 1) * BLOCK, :].T
        xt_ref[b] = block
        full_ref[:, b * BLOCK : (b + 1) * BLOCK] = block
    ids = sub_iota(BLOCK, BF)
    for rows, out_ref in zip(list_order(core_ref[0], rows_ref), out_refs):
        for g in range(length // BLOCK):
            row = rows[:, g * BLOCK : (g + 1) * BLOCK]
            for b in range(blocks):
                hot_ref[b * BLOCK : (b + 1) * BLOCK, g * BLOCK : (g + 1) * BLOCK] = onehot_t(
                    (row - b * BLOCK).astype(F32), ids
                )
        out_ref[...] = mm(full_ref[...], hot_ref[...]).T.astype(BF)


def main_kernel(
    src_ref, core_ref, xt_loc_ref, r0_ref, r1_ref, r2_ref, r3_ref, book_ref, cell_ref, w_ref, dw_ref, cg_ref,
    coarse_ref, pg_ref, wt_ref, keep_ref, give_ref,
    xt_ref, gt_ref, conv_ref, sg_ref, ch_ref, part_ref,
):
    kvol = w_ref.shape[0]
    blocks = xt_loc_ref.shape[0]
    recv_refs = (r0_ref, r1_ref, r2_ref, r3_ref)
    each = r0_ref.shape[0] // BLOCK
    far = 4 * each
    child = dw_ref.shape[0]
    quarter = cg_ref.shape[0] // blocks
    ids = sub_iota(BLOCK, BF)
    ids2 = jnp.concatenate([ids, ids + jnp.asarray(BLOCK, BF)], axis=0)

    for k in range(kvol):
        wt_ref[:, k * BLOCK : (k + 1) * BLOCK] = w_ref[k].T
    for b in range(blocks):
        xt_ref[b] = xt_loc_ref[b]
    for b in range(far):
        one = b % each
        slot = slot_order(core_ref[0])[b // each]
        xt_ref[blocks + each * slot + one] = recv_refs[b // each][one * BLOCK : (one + 1) * BLOCK, :].T
    xt_ref[blocks + far] = jnp.zeros((BLOCK, BLOCK), BF)
    for j in range(child):
        part = mm(cg_ref[...], dw_ref[j], NT).astype(BF)
        for b in range(blocks):
            sg_ref[b, j * quarter : (j + 1) * quarter, :] = part[b * quarter : (b + 1) * quarter, :]
    conv_ref[...] = jnp.zeros_like(conv_ref)

    @pl.loop(0, blocks // 2)
    def _(p):
        for k in range(kvol):
            for h in range(2):
                b = 2 * p + h
                hot = onehot_t(book_ref[b, k : k + 1, :], ids)
                got = mm(xt_ref[src_ref[k, b]], hot)
                gt_ref[k * BLOCK : (k + 1) * BLOCK, h * BLOCK : (h + 1) * BLOCK] = got.astype(BF)
        pre = mm(wt_ref[...], gt_ref[...])
        hid = jnp.maximum(pre, 0.0).astype(BF)
        halves = []
        for h in range(2):
            b = 2 * p + h
            hot = onehot_t(cell_ref[pl.ds(b, 1), :], ids2)
            kids = mm(hot, hid[:, h * BLOCK : (h + 1) * BLOCK], NT).astype(BF)
            for j in range(child):
                ch_ref[pl.ds(pl.multiple_of(b * quarter, quarter), quarter), j * BLOCK : (j + 1) * BLOCK] = (
                    kids[j * quarter : (j + 1) * quarter, :]
                )
            halves.append(mm(sg_ref[b], hot, TN))
        grad = jnp.concatenate(halves, axis=1)
        pgt = jnp.where(pre > 0, grad, 0.0).astype(BF)
        pg = pgt.T
        pg_ref[p] = pg
        conv_ref[...] += mm(gt_ref[...], pg)

    kids = ch_ref[...]
    coarse_ref[...] = mm(kids, dw_ref[...].reshape(child * BLOCK, BLOCK)).astype(BF)
    rows = kvol * BLOCK
    part_ref[0:rows, :] = conv_ref[...].astype(BF)
    part_ref[rows : rows + child * BLOCK, :] = mm(kids, cg_ref[...], TN).astype(BF)
    rest = part_ref.shape[0] - rows - child * BLOCK
    part_ref[rows + child * BLOCK :, :] = jnp.zeros((rest, BLOCK), BF)
    half = keep_ref.shape[0]
    core = core_ref[0]
    keep_ref[...] = part_ref[pl.ds(pl.multiple_of(core * half, half), half), :]
    give_ref[...] = part_ref[pl.ds(pl.multiple_of((1 - core) * half, half), half), :]


def back_kernel(lo, hi, pairs, src_ref, core_ref, book_ref, wt_ref, pg_ref, *refs):
    refs, back_ref = refs[:-1], refs[-1]
    if lo > 0:
        before_ref, refs = refs[0], refs[1:]
    if hi < pairs:
        (table_ref,) = refs
    else:
        local_ref, *far_refs, table_ref = refs
    table_ref[...] = jnp.zeros_like(table_ref) if lo == 0 else before_ref[...]
    kvol = book_ref.shape[1]
    ids = sub_iota(BLOCK, BF)

    @pl.loop(lo, hi)
    def _(p):
        back_ref[...] = mm(pg_ref[p], wt_ref[...]).astype(BF)
        for k in range(kvol):
            for h in range(2):
                b = 2 * p + h
                hot = onehot_t(book_ref[b, k : k + 1, :], ids)
                table_ref[src_ref[k, b]] += mm(
                    hot, back_ref[h * BLOCK : (h + 1) * BLOCK, k * BLOCK : (k + 1) * BLOCK]
                )

    if hi == pairs:
        blocks = local_ref.shape[0] // BLOCK
        for b in range(blocks):
            local_ref[b * BLOCK : (b + 1) * BLOCK, :] = table_ref[b]
        for slot, far_ref in zip(slot_order(core_ref[0]), far_refs):
            each = far_ref.shape[0] // BLOCK
            for one in range(each):
                far_ref[one * BLOCK : (one + 1) * BLOCK, :] = table_ref[blocks + each * slot + one].astype(BF)


def add_kernel(info_ref, local_ref, rows_ref, g0_ref, g1_ref, g2_ref, g3_ref, out_ref, ret_ref):
    blocks = out_ref.shape[0] // BLOCK
    length = rows_ref.shape[1]
    ids = sub_iota(BLOCK, BF)
    nothing = jnp.zeros((length, BLOCK), BF)
    slab = info_ref[1]
    ret_ref[0:length, :] = jnp.where(slab < info_ref[2] - 1, g0_ref[...], nothing)
    ret_ref[length : 2 * length, :] = jnp.where(slab > 0, g1_ref[...], nothing)
    ret_ref[2 * length : 3 * length, :] = g2_ref[...]
    ret_ref[3 * length :, :] = g3_ref[...]
    groups = [
        rows[:, g * BLOCK : (g + 1) * BLOCK]
        for rows in list_order(info_ref[0], rows_ref)
        for g in range(length // BLOCK)
    ]
    for b in range(blocks):
        hot = jnp.concatenate([onehot_t((row - b * BLOCK).astype(F32), ids) for row in groups], axis=1)
        spot = slice(b * BLOCK, (b + 1) * BLOCK)
        out_ref[spot, :] = local_ref[spot, :] + mm(hot, ret_ref[...])


def spread_kernel(core_ref, own_ref, other_ref, conv_ref, down_ref):
    half = own_ref.shape[0]
    rows = conv_ref.shape[0]

    def put(low_ref, high_ref):
        conv_ref[0:half, :] = low_ref[...].astype(F32)
        conv_ref[half:rows, :] = high_ref[0 : rows - half, :].astype(F32)
        down_ref[...] = high_ref[rows - half : rows - half + down_ref.shape[0], :].astype(F32)

    @pl.when(core_ref[0] == 0)
    def _():
        put(own_ref, other_ref)

    @pl.when(core_ref[0] != 0)
    def _():
        put(other_ref, own_ref)


def here(x):
    return pltpu.with_memory_space_constraint(x, pltpu.VMEM)


def call(kernel, outs, ins, scratch=(), aliases=None):
    single = len(outs) == 1
    shapes = tuple((jax.ShapeDtypeStruct if not near else pltpu.VMEM)(s, d) for s, d, *near in outs)
    return pl.pallas_call(
        kernel,
        out_shape=shapes[0] if single else shapes,
        in_specs=ins,
        out_specs=VM if single else tuple(VM for _ in outs),
        scratch_shapes=list(scratch),
        input_output_aliases=aliases or {},
        compiler_params=pltpu.CompilerParams(vmem_limit_bytes=VMEM_LIMIT),
    )


def wide(v):
    return v.astype(F32)


def tie(*values):
    return lax.optimization_barrier(values)


def body(features, conv_weight, down_weight, coarse_grad, rulebook, boundary_rows, parent_code):
    row_count, chans = features.shape
    coarse_rows, out_chans = coarse_grad.shape
    list_len = boundary_rows.shape[1]
    child = down_weight.shape[0]
    kvol = conv_weight.shape[0]
    blocks = row_count // BLOCK
    pairs = blocks // 2
    far_rows = 4 * list_len
    quarter = coarse_rows // blocks
    slabs, tiles = lax.axis_size("slab"), lax.axis_size("tile")
    place = lax.axis_index("slab") * tiles + lax.axis_index("tile")
    core = place & 1
    info = jnp.stack([core, lax.axis_index("slab"), jnp.int32(slabs)])

    near = True
    *outgoing, xt = call(
        pick_kernel,
        [((list_len, chans), BF, near)] * 4 + [((blocks, BLOCK, BLOCK), BF, near)],
        [SM, VM, VM],
        [pltpu.VMEM((BLOCK, row_count), BF), pltpu.VMEM((row_count, list_len), BF)],
    )(info, features, boundary_rows)
    up = [(i, i + 1) for i in range(slabs - 1)]
    down = [(i + 1, i) for i in range(slabs - 1)]
    chip = [(i, i ^ 1) for i in range(tiles)]
    beside = [(i, i + 2 * (i % 2) - 1) for i in range(1, tiles - 1)]
    received = [
        lax.ppermute(outgoing[0], "slab", up),
        lax.ppermute(outgoing[1], "slab", down),
        lax.ppermute(outgoing[2], "tile", chip),
        lax.ppermute(outgoing[3], "tile", beside),
    ]
    source, inner, cell = call(
        index_kernel,
        [((kvol, BLOCK), jnp.int32), ((blocks, kvol, BLOCK), F32, near), ((blocks, BLOCK), F32, near)],
        [VM, VM],
    )(rulebook, parent_code.reshape(1, row_count))

    grad_rows = (kvol + child) * BLOCK
    part_rows = -(-grad_rows // 512) * 512
    table = blocks + far_rows // BLOCK + 1
    coarse, pg, wt, keep, give = call(
        main_kernel,
        [
            ((coarse_rows, out_chans), BF),
            ((pairs, 2 * BLOCK, BLOCK), BF, near),
            ((BLOCK, kvol * BLOCK), BF, near),
            ((part_rows // 2, out_chans), BF, near),
            ((part_rows // 2, out_chans), BF, near),
        ],
        [SM, SM] + [VM] * 10,
        [
            pltpu.VMEM((table, BLOCK, BLOCK), BF),
            pltpu.VMEM((kvol * BLOCK, 2 * BLOCK), BF),
            pltpu.VMEM((kvol * BLOCK, BLOCK), F32),
            pltpu.VMEM((blocks, child * quarter, BLOCK), BF),
            pltpu.VMEM((coarse_rows, child * BLOCK), BF),
            pltpu.VMEM((part_rows, BLOCK), BF),
        ],
    )(source, info, here(xt), *map(here, received), here(inner), here(cell), conv_weight, down_weight, coarse_grad)

    def back_part(acc, lo, hi):
        ins = (source, info, here(inner), here(wt), here(pg)) + (() if acc is None else (here(acc),))
        whole = ((table, BLOCK, BLOCK), F32, near)
        scratch = [pltpu.VMEM((2 * BLOCK, kvol * BLOCK), BF)]
        if hi < pairs:
            outs = [whole]
        else:
            outs = [((row_count, chans), F32, near)] + [((list_len, chans), BF, near)] * 4
            scratch = [pltpu.VMEM(*whole[:2])] + scratch
        return call(
            functools.partial(back_kernel, lo, hi, pairs), outs, [SM, SM] + [VM] * (len(ins) - 2), scratch
        )(*ins)

    stride = {"c": 1, "z": 2, "y": 8, "x": tiles}
    size = {"c": 2, "z": 4, "y": tiles // 8, "x": slabs}

    def send(v, axes, to):
        links = []
        for i in range(slabs * tiles):
            axis = axes[i % 2]
            st, n = stride[axis], size[axis]
            q = (i // st) % n
            links.append((i, i + (to(q) % n - q) * st))
        return lax.ppermute(v, ("slab", "tile"), links)

    def spot(axes):
        first, second = [(place >> (stride[a].bit_length() - 1)) & (size[a] - 1) for a in axes]
        return jnp.where(core == 0, first, second)

    def shifts(axes, pieces):
        return [send(v, axes, lambda q, sh=sh: q + sh) for sh, v in zip((1, 2, 3), pieces)]

    order = ("xx", "yz", "zy", "xx")
    swap = send(give, "cc", lambda q: 1 - q)
    acc = back_part(None, 0, 2)
    swap, acc = tie(swap, acc)
    y = (wide(keep) + wide(swap)).astype(BF)

    i, m = spot(order[0]), y.shape[0] // 4
    mine = lax.dynamic_slice_in_dim(y, i * m, m, 0)
    got = shifts(order[0], [lax.dynamic_slice_in_dim(y, ((i + sh) & 3) * m, m, 0) for sh in (1, 2, 3)])
    acc = back_part(acc, 2, 4)
    *got, acc = tie(*got, acc)
    y = ((wide(mine) + wide(got[1])) + (wide(got[0]) + wide(got[2]))).astype(BF)

    for ph, (lo, hi) in ((1, (4, 6)), (2, (6, 8))):
        y, acc = tie(y, acc)
        got = shifts(order[ph], [y] * 3)
        result = back_part(acc, lo, hi)
        if hi < pairs:
            acc = result
            *got, acc = tie(*got, acc)
        else:
            *got, local, far0, far1, far2, far3 = tie(*got, *result)
        y = ((wide(y) + wide(got[1])) + (wide(got[0]) + wide(got[2]))).astype(BF)

    i = spot(order[3])
    got = shifts(order[3], [jnp.concatenate([y, far1]), y, jnp.concatenate([y, far0])])
    returned = [
        got[2][m:],
        got[0][m:],
        lax.ppermute(far2, "tile", chip),
        lax.ppermute(far3, "tile", beside),
    ]
    got = [got[0][:m], got[1], got[2][:m]]
    full = jnp.zeros((4 * m, out_chans), BF)
    for sh, v in zip((0, 1, 2, 3), [y] + got):
        full = lax.dynamic_update_slice_in_dim(full, v, ((i + 4 - sh) & 3) * m, 0)
    other = send(full, "cc", lambda q: 1 - q)
    input_grad = call(
        add_kernel, [((row_count, chans), F32)], [SM] + [VM] * 6, [pltpu.VMEM((far_rows, chans), BF)]
    )(info, here(local), boundary_rows, *map(here, returned))
    conv_grad, down_grad = call(
        spread_kernel,
        [((kvol * BLOCK, out_chans), F32), ((child * BLOCK, out_chans), F32)],
        [SM, VM, VM],
    )(info, here(full), here(other))
    return (
        coarse,
        input_grad,
        conv_grad.reshape(kvol, chans, chans),
        down_grad.reshape(child, chans, out_chans),
    )


def solution(mesh):
    return jax.shard_map(
        body,
        mesh=mesh,
        in_specs=(
            P(("slab", "tile"), None),
            P(),
            P(),
            P(("slab", "tile"), None),
            P(None, ("slab", "tile")),
            P(("slab", "tile"), None),
            P(("slab", "tile")),
        ),
        out_specs=(P(("slab", "tile"), None), P(("slab", "tile"), None), P(), P()),
        check_vma=False,
    )
```

```python
import functools

import jax
import jax.numpy as jnp
from jax import lax
from jax.experimental import pallas as pl
from jax.experimental.pallas import tpu as pltpu
from jax.sharding import PartitionSpec as P

BLOCK = 128
BF = jnp.bfloat16
F32 = jnp.float32
VM = pl.BlockSpec(memory_space=pltpu.VMEM)
SM = pl.BlockSpec(memory_space=pltpu.SMEM)

NN = (((1,), (0,)), ((), ()))
NT = (((1,), (1,)), ((), ()))
TN = (((0,), (0,)), ((), ()))


def mm(a, b, dims=NN):
    return lax.dot_general(a, b, dims, preferred_element_type=F32)


def sub_iota(rows, dtype=F32):
    return lax.broadcasted_iota(jnp.int32, (rows, BLOCK), 0).astype(F32).astype(dtype)


def onehot_t(row, ids):
    wide = jnp.broadcast_to(row, (16, BLOCK)).astype(BF)
    wide = jnp.concatenate([wide] * (ids.shape[0] // 16), axis=0)
    return jnp.where(ids == wide, jnp.ones((), BF), jnp.zeros((), BF))


def core_id():
    return lax.axis_index("tile") & 1


def list_order(core, rows_ref):
    rows = [rows_ref[d : d + 1, :] for d in range(4)]
    return (rows[0], rows[1], jnp.where(core == 0, rows[2], rows[3]), jnp.where(core == 0, rows[3], rows[2]))


def slot_order(core):
    return (0, 1, 3 - core, 2 + core)


def index_kernel(book_ref, code_ref, w_ref, dw_ref, cg_ref, src_ref, inner_ref, cell_ref, wt_ref, sg_ref):
    kvol = book_ref.shape[0]
    blocks, child, quarter = cell_ref.shape[0], 8, BLOCK // 4
    lane = lax.broadcasted_iota(jnp.int32, (kvol, BLOCK), 1)
    found = jnp.zeros((kvol, BLOCK), jnp.int32)
    for b in range(blocks):
        book = book_ref[:, b * BLOCK : (b + 1) * BLOCK]
        block = jnp.min(book, axis=1, keepdims=True) // BLOCK
        inner_ref[b] = (book - block * BLOCK).astype(F32)
        found = jnp.where(lane == b, block, found)
        code = code_ref[:, b * BLOCK : (b + 1) * BLOCK]
        cell = (code % child) * quarter + code // child - b * quarter
        cell_ref[b : b + 1, :] = jnp.where(code < child * quarter * blocks, cell, -1).astype(F32)
    src_ref[...] = found
    for k in range(kvol):
        wt_ref[:, k * BLOCK : (k + 1) * BLOCK] = w_ref[k].T
    for j in range(child):
        part = mm(cg_ref[...], dw_ref[j], NT).astype(BF)
        for b in range(blocks):
            sg_ref[b, j * quarter : (j + 1) * quarter, :] = part[b * quarter : (b + 1) * quarter, :]


def pick_kernel(feat_ref, rows_ref, *refs):
    out_refs, xt_ref, full_ref, hot_ref = refs[:-3], refs[-3], refs[-2], refs[-1]
    blocks = feat_ref.shape[0] // BLOCK
    length = rows_ref.shape[1]
    for b in range(blocks):
        block = feat_ref[b * BLOCK : (b + 1) * BLOCK, :].T
        xt_ref[b] = block
        full_ref[:, b * BLOCK : (b + 1) * BLOCK] = block
    ids = sub_iota(BLOCK, BF)
    for rows, out_ref in zip(list_order(core_id(), rows_ref), out_refs):
        for g in range(length // BLOCK):
            row = rows[:, g * BLOCK : (g + 1) * BLOCK]
            for b in range(blocks):
                hot_ref[b * BLOCK : (b + 1) * BLOCK, g * BLOCK : (g + 1) * BLOCK] = onehot_t(
                    (row - b * BLOCK).astype(F32), ids
                )
        out_ref[...] = mm(full_ref[...], hot_ref[...]).T.astype(BF)


def main_kernel(
    src_ref, xt_loc_ref, r0_ref, r1_ref, r2_ref, r3_ref, book_ref, cell_ref, wt_ref, sg_ref, dw_ref, cg_ref,
    coarse_ref, pg_ref, keep_ref, give_ref,
    xt_ref, gt_ref, ch_ref, part_ref,
):
    kvol = book_ref.shape[1]
    blocks = xt_loc_ref.shape[0]
    recv_refs = (r0_ref, r1_ref, r2_ref, r3_ref)
    each = r0_ref.shape[0] // BLOCK
    far = 4 * each
    child = dw_ref.shape[0]
    quarter = cg_ref.shape[0] // blocks
    ids = sub_iota(BLOCK, BF)
    ids2 = jnp.concatenate([ids, ids + jnp.asarray(BLOCK, BF)], axis=0)

    for b in range(blocks):
        xt_ref[b] = xt_loc_ref[b]
    for b in range(far):
        one = b % each
        slot = slot_order(core_id())[b // each]
        xt_ref[blocks + each * slot + one] = recv_refs[b // each][one * BLOCK : (one + 1) * BLOCK, :].T
    xt_ref[blocks + far] = jnp.zeros((BLOCK, BLOCK), BF)
    ch_ref[(blocks - 1) * quarter :, :] = jnp.zeros((quarter, child * BLOCK), BF)
    pg_ref[blocks // 2 - 1, BLOCK:, :] = jnp.zeros((BLOCK, BLOCK), BF)

    def some(p, count):
        for k in range(kvol):
            for h in range(count):
                b = 2 * p + h
                hot = onehot_t(book_ref[b, k : k + 1, :], ids)
                got = mm(xt_ref[src_ref[k, b]], hot)
                at = pl.multiple_of(p * 2 * BLOCK + h * BLOCK, BLOCK)
                gt_ref[k * BLOCK : (k + 1) * BLOCK, pl.ds(at, BLOCK)] = got.astype(BF)
        width = count * BLOCK
        pre = mm(wt_ref[...], gt_ref[:, pl.ds(pl.multiple_of(p * 2 * BLOCK, 2 * BLOCK), width)])
        hid = jnp.maximum(pre, 0.0).astype(BF)
        halves = []
        for h in range(count):
            b = 2 * p + h
            hot = onehot_t(cell_ref[pl.ds(b, 1), :], ids2)
            kids = mm(hot, hid[:, h * BLOCK : (h + 1) * BLOCK], NT).astype(BF)
            for j in range(child):
                ch_ref[pl.ds(pl.multiple_of(b * quarter, quarter), quarter), j * BLOCK : (j + 1) * BLOCK] = (
                    kids[j * quarter : (j + 1) * quarter, :]
                )
            halves.append(mm(sg_ref[b], hot, TN))
        grad = jnp.concatenate(halves, axis=1)
        pgt = jnp.where(pre > 0, grad, 0.0).astype(BF)
        pg_ref[p, 0:width, :] = pgt.T

    @pl.loop(0, blocks // 2 - 1)
    def _(p):
        some(p, 2)

    some(blocks // 2 - 1, 1)
    live = (blocks - 1) * BLOCK
    conv = mm(gt_ref[:, 0:live], pg_ref[...].reshape(blocks * BLOCK, BLOCK)[0:live, :])

    kids = ch_ref[...]
    coarse_ref[...] = mm(kids, dw_ref[...].reshape(child * BLOCK, BLOCK)).astype(BF)
    rows = kvol * BLOCK
    part_ref[0:rows, :] = conv.astype(BF)
    part_ref[rows : rows + child * BLOCK, :] = mm(kids, cg_ref[...], TN).astype(BF)
    rest = part_ref.shape[0] - rows - child * BLOCK
    part_ref[rows + child * BLOCK :, :] = jnp.zeros((rest, BLOCK), BF)
    half = keep_ref.shape[0]
    core = core_id()
    keep_ref[...] = part_ref[pl.ds(pl.multiple_of(core * half, half), half), :]
    give_ref[...] = part_ref[pl.ds(pl.multiple_of((1 - core) * half, half), half), :]


def back_kernel(lo, hi, pairs, src_ref, book_ref, wt_ref, pg_ref, *refs):
    refs, back_ref = refs[:-1], refs[-1]
    if lo > 0:
        before_ref, refs = refs[0], refs[1:]
    if hi < pairs:
        (table_ref,) = refs
    else:
        local_ref, *far_refs, table_ref = refs
    table_ref[...] = jnp.zeros_like(table_ref) if lo == 0 else before_ref[...]
    kvol = book_ref.shape[1]
    ids = sub_iota(BLOCK, BF)

    def some(p, count):
        back_ref[0 : count * BLOCK, :] = mm(pg_ref[p, 0 : count * BLOCK, :], wt_ref[...]).astype(BF)
        for k in range(kvol):
            for h in range(count):
                b = 2 * p + h
                hot = onehot_t(book_ref[b, k : k + 1, :], ids)
                table_ref[src_ref[k, b]] += mm(
                    hot, back_ref[h * BLOCK : (h + 1) * BLOCK, k * BLOCK : (k + 1) * BLOCK]
                )

    @pl.loop(lo, min(hi, pairs - 1))
    def _(p):
        some(p, 2)

    if hi == pairs:
        some(pairs - 1, 1)
        blocks = local_ref.shape[0] // BLOCK
        for b in range(blocks):
            local_ref[b * BLOCK : (b + 1) * BLOCK, :] = table_ref[b]
        for slot, far_ref in zip(slot_order(core_id()), far_refs):
            each = far_ref.shape[0] // BLOCK
            for one in range(each):
                far_ref[one * BLOCK : (one + 1) * BLOCK, :] = table_ref[blocks + each * slot + one].astype(BF)


def add_kernel(local_ref, rows_ref, g0_ref, g1_ref, g2_ref, g3_ref, out_ref, ret_ref):
    blocks = out_ref.shape[0] // BLOCK
    length = rows_ref.shape[1]
    ids = sub_iota(BLOCK, BF)
    nothing = jnp.zeros((length, BLOCK), BF)
    slab = lax.axis_index("slab")
    ret_ref[0:length, :] = jnp.where(slab < lax.axis_size("slab") - 1, g0_ref[g0_ref.shape[0] - length :, :], nothing)
    ret_ref[length : 2 * length, :] = jnp.where(slab > 0, g1_ref[g1_ref.shape[0] - length :, :], nothing)
    ret_ref[2 * length : 3 * length, :] = g2_ref[...]
    ret_ref[3 * length :, :] = g3_ref[...]
    groups = [
        rows[:, g * BLOCK : (g + 1) * BLOCK]
        for rows in list_order(core_id(), rows_ref)
        for g in range(length // BLOCK)
    ]
    for b in range(blocks):
        hot = jnp.concatenate([onehot_t((row - b * BLOCK).astype(F32), ids) for row in groups], axis=1)
        spot = slice(b * BLOCK, (b + 1) * BLOCK)
        out_ref[spot, :] = local_ref[spot, :] + mm(hot, ret_ref[...])


def wide(v):
    return v.astype(F32)


def quarter_at(n, m):
    return pl.ds(pl.multiple_of((n & 3) * m, m), m)


def pair_kernel(keep_ref, swap_ref, mine_ref, *piece_refs):
    m = mine_ref.shape[0]
    slab = lax.axis_index("slab")
    for sh, out_ref in enumerate((mine_ref, *piece_refs)):
        at = quarter_at(slab + sh, m)
        out_ref[...] = (wide(keep_ref[at, :]) + wide(swap_ref[at, :])).astype(BF)


def four_kernel(own_ref, g1_ref, g2_ref, g3_ref, *refs):
    outs = refs[0:1] if len(refs) == 1 else refs[2:]
    total = (wide(own_ref[...]) + wide(g2_ref[...])) + (wide(g1_ref[...]) + wide(g3_ref[...]))
    m = own_ref.shape[0]
    for out_ref in outs:
        out_ref[0:m, :] = total.astype(BF)
    if len(outs) > 1:
        outs[1][m:, :] = refs[0][...]
        outs[2][m:, :] = refs[1][...]


def join_kernel(own_ref, g1_ref, g2_ref, g3_ref, full_ref):
    m = own_ref.shape[0]
    slab = lax.axis_index("slab") + 4
    for sh, ref in enumerate((own_ref, g1_ref, g2_ref, g3_ref)):
        full_ref[quarter_at(slab - sh, m), :] = ref[0:m, :]


def spread_kernel(own_ref, other_ref, conv_ref, down_ref):
    half = own_ref.shape[0]
    rows = conv_ref.shape[0]

    def put(low_ref, high_ref):
        conv_ref[0:half, :] = low_ref[...].astype(F32)
        conv_ref[half:rows, :] = high_ref[0 : rows - half, :].astype(F32)
        down_ref[...] = high_ref[rows - half : rows - half + down_ref.shape[0], :].astype(F32)

    @pl.when(core_id() == 0)
    def _():
        put(own_ref, other_ref)

    @pl.when(core_id() != 0)
    def _():
        put(other_ref, own_ref)


def here(x):
    return pltpu.with_memory_space_constraint(x, pltpu.VMEM)


def afar(x):
    return pltpu.with_memory_space_constraint(x, pltpu.HBM)


def call(mib, kernel, outs, ins, scratch=()):
    single = len(outs) == 1
    shapes = tuple((jax.ShapeDtypeStruct if not near else pltpu.VMEM)(s, d) for s, d, *near in outs)
    return pl.pallas_call(
        kernel,
        out_shape=shapes[0] if single else shapes,
        in_specs=ins,
        out_specs=VM if single else tuple(VM for _ in outs),
        scratch_shapes=list(scratch),
        compiler_params=pltpu.CompilerParams(vmem_limit_bytes=mib * 1024 * 1024),
    )


def tie(*values):
    return lax.optimization_barrier(values)


def body(features, conv_weight, down_weight, coarse_grad, rulebook, boundary_rows, parent_code):
    row_count, chans = features.shape
    coarse_rows, out_chans = coarse_grad.shape
    list_len = boundary_rows.shape[1]
    child = down_weight.shape[0]
    kvol = conv_weight.shape[0]
    blocks = row_count // BLOCK
    pairs = blocks // 2
    far_rows = 4 * list_len
    quarter = coarse_rows // blocks
    slabs, tiles = lax.axis_size("slab"), lax.axis_size("tile")
    place = lax.axis_index("slab") * tiles + lax.axis_index("tile")
    core = place & 1

    near = True
    *outgoing, xt = call(
        12,
        pick_kernel,
        [((list_len, chans), BF, near)] * 4 + [((blocks, BLOCK, BLOCK), BF, near)],
        [VM, VM],
        [pltpu.VMEM((BLOCK, row_count), BF), pltpu.VMEM((row_count, list_len), BF)],
    )(afar(features), afar(boundary_rows))
    up = [(i, i + 1) for i in range(slabs - 1)]
    down = [(i + 1, i) for i in range(slabs - 1)]
    chip = [(i, i ^ 1) for i in range(tiles)]
    beside = [(i, i + 2 * (i % 2) - 1) for i in range(1, tiles - 1)]
    received = [
        lax.ppermute(outgoing[0], "slab", up),
        lax.ppermute(outgoing[1], "slab", down),
        lax.ppermute(outgoing[2], "tile", chip),
        lax.ppermute(outgoing[3], "tile", beside),
    ]
    source, inner, cell, wt, sg = call(
        12,
        index_kernel,
        [
            ((kvol, BLOCK), jnp.int32),
            ((blocks, kvol, BLOCK), F32, near),
            ((blocks, BLOCK), F32, near),
            ((BLOCK, kvol * BLOCK), BF, near),
            ((blocks, child * quarter, BLOCK), BF, near),
        ],
        [VM] * 5,
    )(*map(afar, (rulebook, parent_code.reshape(1, row_count), conv_weight, down_weight, coarse_grad)))

    grad_rows = (kvol + child) * BLOCK
    part_rows = -(-grad_rows // 512) * 512
    table = blocks + far_rows // BLOCK + 1
    coarse, pg, keep, give = call(
        32,
        main_kernel,
        [
            ((coarse_rows, out_chans), BF),
            ((pairs, 2 * BLOCK, BLOCK), BF, near),
            ((part_rows // 2, out_chans), BF, near),
            ((part_rows // 2, out_chans), BF, near),
        ],
        [SM] + [VM] * 11,
        [
            pltpu.VMEM((table, BLOCK, BLOCK), BF),
            pltpu.VMEM((kvol * BLOCK, row_count), BF),
            pltpu.VMEM((coarse_rows, child * BLOCK), BF),
            pltpu.VMEM((part_rows, BLOCK), BF),
        ],
    )(source, *map(here, (xt, *received, inner, cell, wt, sg)), afar(down_weight), afar(coarse_grad))

    def back_part(acc, lo, hi):
        ins = (source, here(inner), here(wt), here(pg)) + (() if acc is None else (here(acc),))
        whole = ((table, BLOCK, BLOCK), F32, near)
        scratch = [pltpu.VMEM((2 * BLOCK, kvol * BLOCK), BF)]
        if hi < pairs:
            outs = [whole]
        else:
            outs = [((row_count, chans), F32, near)] + [((list_len, chans), BF, near)] * 4
            scratch = [pltpu.VMEM(*whole[:2])] + scratch
        return call(
            12, functools.partial(back_kernel, lo, hi, pairs), outs, [SM] + [VM] * (len(ins) - 1), scratch
        )(*ins)

    stride = {"c": 1, "z": 2, "y": 8, "x": tiles}
    size = {"c": 2, "z": 4, "y": tiles // 8, "x": slabs}

    def send(v, axes, to):
        links = []
        for i in range(slabs * tiles):
            axis = axes[i % 2]
            st, n = stride[axis], size[axis]
            q = (i // st) % n
            links.append((i, i + (to(q) % n - q) * st))
        return lax.ppermute(v, ("slab", "tile"), links)

    def shifts(axes, pieces):
        return [send(v, axes, lambda q, sh=sh: q + sh) for sh, v in zip((1, 2, 3), pieces)]

    order = ("xx", "yz", "zy", "xx")
    swap = send(give, "cc", lambda q: 1 - q)
    acc = back_part(None, 0, 2)
    swap, acc = tie(swap, acc)
    m = part_rows // 8
    near_piece = ((m, out_chans), BF, near)
    long_piece = ((m + list_len, out_chans), BF, near)
    y, *pieces = call(8, pair_kernel, [near_piece] * 4, [VM] * 2)(here(keep), here(swap))

    for ph, (lo, hi) in enumerate(((2, 4), (4, 6), (6, 8))):
        y, acc = tie(y, acc)
        got = shifts(order[ph], pieces)
        result = back_part(acc, lo, hi)
        if hi < pairs:
            acc = result
            *got, acc = tie(*got, acc)
            y = call(8, four_kernel, [near_piece], [VM] * 4)(*map(here, (y, *got)))
            pieces = [y] * 3
        else:
            *got, local, far0, far1, far2, far3 = tie(*got, *result)
            y, low, high = call(8, four_kernel, [near_piece, long_piece, long_piece], [VM] * 6)(
                *map(here, (y, *got, far0, far1))
            )

    got = shifts(order[3], [high, y, low])
    returned = [
        got[2],
        got[0],
        lax.ppermute(far2, "tile", chip),
        lax.ppermute(far3, "tile", beside),
    ]
    full = call(8, join_kernel, [((4 * m, out_chans), BF, near)], [VM] * 4)(*map(here, (y, *got)))
    other = send(full, "cc", lambda q: 1 - q)
    input_grad = call(
        12, add_kernel, [((row_count, chans), F32)], [VM] * 6, [pltpu.VMEM((far_rows, chans), BF)]
    )(here(local), afar(boundary_rows), *map(here, returned))
    conv_grad, down_grad = call(
        12,
        spread_kernel,
        [((kvol * BLOCK, out_chans), F32), ((child * BLOCK, out_chans), F32)],
        [VM, VM],
    )(here(full), here(other))
    return (
        coarse,
        input_grad,
        conv_grad.reshape(kvol, chans, chans),
        down_grad.reshape(child, chans, out_chans),
    )


def solution(mesh):
    return jax.shard_map(
        body,
        mesh=mesh,
        in_specs=(
            P(("slab", "tile"), None),
            P(),
            P(),
            P(("slab", "tile"), None),
            P(None, ("slab", "tile")),
            P(("slab", "tile"), None),
            P(("slab", "tile")),
        ),
        out_specs=(P(("slab", "tile"), None), P(("slab", "tile"), None), P(), P()),
        check_vma=False,
    )
```

```python
import functools

import jax
import jax.numpy as jnp
from jax import lax
from jax.experimental import pallas as pl
from jax.experimental.pallas import tpu as pltpu
from jax.sharding import PartitionSpec as P

BLOCK = 128
BF = jnp.bfloat16
F32 = jnp.float32
VM = pl.BlockSpec(memory_space=pltpu.VMEM)
SM = pl.BlockSpec(memory_space=pltpu.SMEM)

NN = (((1,), (0,)), ((), ()))
NT = (((1,), (1,)), ((), ()))
TN = (((0,), (0,)), ((), ()))


def mm(a, b, dims=NN):
    return lax.dot_general(a, b, dims, preferred_element_type=F32)


def sub_iota(rows, dtype=F32):
    return lax.broadcasted_iota(jnp.int32, (rows, BLOCK), 0).astype(F32).astype(dtype)


def onehot_t(row, ids):
    wide = jnp.broadcast_to(row, (16, BLOCK)).astype(BF)
    wide = jnp.concatenate([wide] * (ids.shape[0] // 16), axis=0)
    return jnp.where(ids == wide, jnp.ones((), BF), jnp.zeros((), BF))


def core_id():
    return lax.axis_index("tile") & 1


def list_order(core, rows_ref):
    rows = [rows_ref[d : d + 1, :] for d in range(4)]
    return (rows[0], rows[1], jnp.where(core == 0, rows[2], rows[3]), jnp.where(core == 0, rows[3], rows[2]))


def slot_order(core):
    return (0, 1, 3 - core, 2 + core)


def index_kernel(book_ref, code_ref, w_ref, dw_ref, cg_ref, src_ref, inner_ref, cell_ref, wt_ref, sg_ref):
    kvol = book_ref.shape[0]
    blocks, child, quarter = cell_ref.shape[0], 8, BLOCK // 4
    lane = lax.broadcasted_iota(jnp.int32, (kvol, BLOCK), 1)
    found = jnp.zeros((kvol, BLOCK), jnp.int32)
    for b in range(blocks):
        book = book_ref[:, b * BLOCK : (b + 1) * BLOCK]
        block = jnp.min(book, axis=1, keepdims=True) // BLOCK
        inner_ref[b] = (book - block * BLOCK).astype(F32)
        found = jnp.where(lane == b, block, found)
        code = code_ref[:, b * BLOCK : (b + 1) * BLOCK]
        cell = (code % child) * quarter + code // child - b * quarter
        cell_ref[b : b + 1, :] = jnp.where(code < child * quarter * blocks, cell, -1).astype(F32)
    src_ref[...] = found
    for k in range(kvol):
        wt_ref[:, k * BLOCK : (k + 1) * BLOCK] = w_ref[k].T
    for j in range(child):
        part = mm(cg_ref[...], dw_ref[j], NT).astype(BF)
        for b in range(blocks):
            sg_ref[b, j * quarter : (j + 1) * quarter, :] = part[b * quarter : (b + 1) * quarter, :]


def pick_kernel(feat_ref, rows_ref, *refs):
    out_refs, xt_ref, full_ref, hot_ref = refs[:-3], refs[-3], refs[-2], refs[-1]
    blocks = feat_ref.shape[0] // BLOCK
    length = rows_ref.shape[1]
    for b in range(blocks):
        block = feat_ref[b * BLOCK : (b + 1) * BLOCK, :].T
        xt_ref[b] = block
        full_ref[:, b * BLOCK : (b + 1) * BLOCK] = block
    ids = sub_iota(BLOCK, BF)
    for rows, out_ref in zip(list_order(core_id(), rows_ref), out_refs):
        for g in range(length // BLOCK):
            row = rows[:, g * BLOCK : (g + 1) * BLOCK]
            for b in range(blocks):
                hot_ref[b * BLOCK : (b + 1) * BLOCK, g * BLOCK : (g + 1) * BLOCK] = onehot_t(
                    (row - b * BLOCK).astype(F32), ids
                )
        out_ref[...] = mm(full_ref[...], hot_ref[...]).T.astype(BF)


def main_kernel(
    src_ref, xt_loc_ref, r0_ref, r1_ref, r2_ref, r3_ref, book_ref, cell_ref, wt_ref, sg_ref, dw_ref, cg_ref,
    coarse_ref, pg_ref, keep_ref, give_ref,
    xt_ref, gt_ref, ch_ref, part_ref,
):
    kvol = book_ref.shape[1]
    blocks = xt_loc_ref.shape[0]
    recv_refs = (r0_ref, r1_ref, r2_ref, r3_ref)
    each = r0_ref.shape[0] // BLOCK
    far = 4 * each
    child = dw_ref.shape[0]
    quarter = cg_ref.shape[0] // blocks
    ids = sub_iota(BLOCK, BF)
    ids2 = jnp.concatenate([ids, ids + jnp.asarray(BLOCK, BF)], axis=0)

    for b in range(blocks):
        xt_ref[b] = xt_loc_ref[b]
    for b in range(far):
        one = b % each
        slot = slot_order(core_id())[b // each]
        xt_ref[blocks + each * slot + one] = recv_refs[b // each][one * BLOCK : (one + 1) * BLOCK, :].T
    xt_ref[blocks + far] = jnp.zeros((BLOCK, BLOCK), BF)
    ch_ref[(blocks - 1) * quarter :, :] = jnp.zeros((quarter, child * BLOCK), BF)
    pg_ref[blocks // 2 - 1, BLOCK:, :] = jnp.zeros((BLOCK, BLOCK), BF)

    def some(p, count):
        for k in range(kvol):
            for h in range(count):
                b = 2 * p + h
                hot = onehot_t(book_ref[b, k : k + 1, :], ids)
                got = mm(xt_ref[src_ref[k, b]], hot)
                at = pl.multiple_of(p * 2 * BLOCK + h * BLOCK, BLOCK)
                gt_ref[k * BLOCK : (k + 1) * BLOCK, pl.ds(at, BLOCK)] = got.astype(BF)
        width = count * BLOCK
        pre = mm(wt_ref[...], gt_ref[:, pl.ds(pl.multiple_of(p * 2 * BLOCK, 2 * BLOCK), width)])
        hid = jnp.maximum(pre, 0.0).astype(BF)
        halves = []
        for h in range(count):
            b = 2 * p + h
            hot = onehot_t(cell_ref[pl.ds(b, 1), :], ids2)
            kids = mm(hot, hid[:, h * BLOCK : (h + 1) * BLOCK], NT).astype(BF)
            for j in range(child):
                ch_ref[pl.ds(pl.multiple_of(b * quarter, quarter), quarter), j * BLOCK : (j + 1) * BLOCK] = (
                    kids[j * quarter : (j + 1) * quarter, :]
                )
            halves.append(mm(sg_ref[b], hot, TN))
        grad = jnp.concatenate(halves, axis=1)
        pgt = jnp.where(pre > 0, grad, 0.0).astype(BF)
        pg_ref[p, 0:width, :] = pgt.T

    @pl.loop(0, blocks // 2 - 1)
    def _(p):
        some(p, 2)

    some(blocks // 2 - 1, 1)
    live = (blocks - 1) * BLOCK
    conv = mm(gt_ref[:, 0:live], pg_ref[...].reshape(blocks * BLOCK, BLOCK)[0:live, :])

    kids = ch_ref[...]
    coarse_ref[...] = mm(kids, dw_ref[...].reshape(child * BLOCK, BLOCK)).astype(BF)
    rows = kvol * BLOCK
    part_ref[0:rows, :] = conv.astype(BF)
    part_ref[rows : rows + child * BLOCK, :] = mm(kids, cg_ref[...], TN).astype(BF)
    rest = part_ref.shape[0] - rows - child * BLOCK
    part_ref[rows + child * BLOCK :, :] = jnp.zeros((rest, BLOCK), BF)
    half = keep_ref.shape[0]
    core = core_id()
    keep_ref[...] = part_ref[pl.ds(pl.multiple_of(core * half, half), half), :]
    give_ref[...] = part_ref[pl.ds(pl.multiple_of((1 - core) * half, half), half), :]


def back_kernel(lo, hi, pairs, src_ref, book_ref, wt_ref, pg_ref, *refs):
    *before_refs, table_ref, back_ref = refs
    table_ref[...] = jnp.zeros_like(table_ref) if lo == 0 else before_refs[0][...]
    kvol = book_ref.shape[1]
    ids = sub_iota(BLOCK, BF)

    def some(p, count):
        back_ref[0 : count * BLOCK, :] = mm(pg_ref[p, 0 : count * BLOCK, :], wt_ref[...]).astype(BF)
        for k in range(kvol):
            for h in range(count):
                b = 2 * p + h
                hot = onehot_t(book_ref[b, k : k + 1, :], ids)
                table_ref[src_ref[k, b]] += mm(
                    hot, back_ref[h * BLOCK : (h + 1) * BLOCK, k * BLOCK : (k + 1) * BLOCK]
                )

    @pl.loop(lo, min(hi, pairs - 1))
    def _(p):
        some(p, 2)

    if hi == pairs:
        some(pairs - 1, 1)


def far_kernel(table_ref, *far_refs):
    each = far_refs[0].shape[0] // BLOCK
    blocks = table_ref.shape[0] - 1 - 4 * each
    for slot, far_ref in zip(slot_order(core_id()), far_refs):
        for one in range(each):
            far_ref[one * BLOCK : (one + 1) * BLOCK, :] = table_ref[blocks + each * slot + one].astype(BF)


def add_kernel(table_ref, rows_ref, g0_ref, g1_ref, g2_ref, g3_ref, out_ref, ret_ref):
    blocks = out_ref.shape[0] // BLOCK
    length = rows_ref.shape[1]
    ids = sub_iota(BLOCK, BF)
    nothing = jnp.zeros((length, BLOCK), BF)
    slab = lax.axis_index("slab")
    ret_ref[0:length, :] = jnp.where(slab < lax.axis_size("slab") - 1, g0_ref[g0_ref.shape[0] - length :, :], nothing)
    ret_ref[length : 2 * length, :] = jnp.where(slab > 0, g1_ref[g1_ref.shape[0] - length :, :], nothing)
    ret_ref[2 * length : 3 * length, :] = g2_ref[...]
    ret_ref[3 * length :, :] = g3_ref[...]
    groups = [
        rows[:, g * BLOCK : (g + 1) * BLOCK]
        for rows in list_order(core_id(), rows_ref)
        for g in range(length // BLOCK)
    ]
    for b in range(blocks):
        hot = jnp.concatenate([onehot_t((row - b * BLOCK).astype(F32), ids) for row in groups], axis=1)
        spot = slice(b * BLOCK, (b + 1) * BLOCK)
        out_ref[spot, :] = table_ref[b] + mm(hot, ret_ref[...])


def wide(v):
    return v.astype(F32)


def first_axis():
    return jnp.where(core_id() == 0, lax.axis_index("slab"), lax.axis_index("tile") >> 3)


def quarter_at(n, m):
    return pl.ds(pl.multiple_of((n & 3) * m, m), m)


def pair_kernel(keep_ref, swap_ref, mine_ref, *piece_refs):
    m = mine_ref.shape[0]
    place = first_axis()
    for sh, out_ref in enumerate((mine_ref, *piece_refs)):
        at = quarter_at(place + sh, m)
        out_ref[...] = (wide(keep_ref[at, :]) + wide(swap_ref[at, :])).astype(BF)


def four_kernel(own_ref, g1_ref, g2_ref, g3_ref, out_ref):
    total = (wide(own_ref[...]) + wide(g2_ref[...])) + (wide(g1_ref[...]) + wide(g3_ref[...]))
    out_ref[...] = total.astype(BF)


def join_kernel(own_ref, g1_ref, g2_ref, g3_ref, full_ref):
    m = own_ref.shape[0]
    place = first_axis() + 4
    for sh, ref in enumerate((own_ref, g1_ref, g2_ref, g3_ref)):
        full_ref[quarter_at(place - sh, m), :] = ref[...]


def spread_kernel(own_ref, other_ref, conv_ref, down_ref):
    half = own_ref.shape[0]
    rows = conv_ref.shape[0]

    def put(low_ref, high_ref):
        conv_ref[0:half, :] = low_ref[...].astype(F32)
        conv_ref[half:rows, :] = high_ref[0 : rows - half, :].astype(F32)
        down_ref[...] = high_ref[rows - half : rows - half + down_ref.shape[0], :].astype(F32)

    @pl.when(core_id() == 0)
    def _():
        put(own_ref, other_ref)

    @pl.when(core_id() != 0)
    def _():
        put(other_ref, own_ref)


def here(x):
    return pltpu.with_memory_space_constraint(x, pltpu.VMEM)


def afar(x):
    return pltpu.with_memory_space_constraint(x, pltpu.HBM)


def call(mib, kernel, outs, ins, scratch=()):
    single = len(outs) == 1
    shapes = tuple((jax.ShapeDtypeStruct if not near else pltpu.VMEM)(s, d) for s, d, *near in outs)
    return pl.pallas_call(
        kernel,
        out_shape=shapes[0] if single else shapes,
        in_specs=ins,
        out_specs=VM if single else tuple(VM for _ in outs),
        scratch_shapes=list(scratch),
        compiler_params=pltpu.CompilerParams(vmem_limit_bytes=mib * 1024 * 1024),
    )


def tie(*values):
    return lax.optimization_barrier(values)


def body(features, conv_weight, down_weight, coarse_grad, rulebook, boundary_rows, parent_code):
    row_count, chans = features.shape
    coarse_rows, out_chans = coarse_grad.shape
    list_len = boundary_rows.shape[1]
    child = down_weight.shape[0]
    kvol = conv_weight.shape[0]
    blocks = row_count // BLOCK
    pairs = blocks // 2
    far_rows = 4 * list_len
    quarter = coarse_rows // blocks
    slabs, tiles = lax.axis_size("slab"), lax.axis_size("tile")
    place = lax.axis_index("slab") * tiles + lax.axis_index("tile")
    core = place & 1

    near = True
    *outgoing, xt = call(
        12,
        pick_kernel,
        [((list_len, chans), BF, near)] * 4 + [((blocks, BLOCK, BLOCK), BF, near)],
        [VM, VM],
        [pltpu.VMEM((BLOCK, row_count), BF), pltpu.VMEM((row_count, list_len), BF)],
    )(afar(features), afar(boundary_rows))
    up = [(i, i + 1) for i in range(slabs - 1)]
    down = [(i + 1, i) for i in range(slabs - 1)]
    chip = [(i, i ^ 1) for i in range(tiles)]
    beside = [(i, i + 2 * (i % 2) - 1) for i in range(1, tiles - 1)]
    received = [
        lax.ppermute(outgoing[0], "slab", up),
        lax.ppermute(outgoing[1], "slab", down),
        lax.ppermute(outgoing[2], "tile", chip),
        lax.ppermute(outgoing[3], "tile", beside),
    ]
    source, inner, cell, wt, sg = call(
        12,
        index_kernel,
        [
            ((kvol, BLOCK), jnp.int32),
            ((blocks, kvol, BLOCK), F32, near),
            ((blocks, BLOCK), F32, near),
            ((BLOCK, kvol * BLOCK), BF, near),
            ((blocks, child * quarter, BLOCK), BF, near),
        ],
        [VM] * 5,
    )(*map(afar, (rulebook, parent_code.reshape(1, row_count), conv_weight, down_weight, coarse_grad)))

    grad_rows = (kvol + child) * BLOCK
    part_rows = -(-grad_rows // 512) * 512
    table = blocks + far_rows // BLOCK + 1
    coarse, pg, keep, give = call(
        32,
        main_kernel,
        [
            ((coarse_rows, out_chans), BF),
            ((pairs, 2 * BLOCK, BLOCK), BF, near),
            ((part_rows // 2, out_chans), BF, near),
            ((part_rows // 2, out_chans), BF, near),
        ],
        [SM] + [VM] * 11,
        [
            pltpu.VMEM((table, BLOCK, BLOCK), BF),
            pltpu.VMEM((kvol * BLOCK, row_count), BF),
            pltpu.VMEM((coarse_rows, child * BLOCK), BF),
            pltpu.VMEM((part_rows, BLOCK), BF),
        ],
    )(source, *map(here, (xt, *received, inner, cell, wt, sg)), afar(down_weight), afar(coarse_grad))

    def back_part(acc, lo, hi):
        ins = (source, here(inner), here(wt), here(pg)) + (() if acc is None else (here(acc),))
        return call(
            12,
            functools.partial(back_kernel, lo, hi, pairs),
            [((table, BLOCK, BLOCK), F32, near)],
            [SM] + [VM] * (len(ins) - 1),
            [pltpu.VMEM((2 * BLOCK, kvol * BLOCK), BF)],
        )(*ins)

    stride = {"c": 1, "z": 2, "y": 8, "x": tiles}
    size = {"c": 2, "z": 4, "y": tiles // 8, "x": slabs}

    def send(v, axes, to):
        links = []
        for i in range(slabs * tiles):
            axis = axes[i % 2]
            st, n = stride[axis], size[axis]
            q = (i // st) % n
            links.append((i, i + (to(q) % n - q) * st))
        return lax.ppermute(v, ("slab", "tile"), links)

    def shifts(axes, pieces):
        sent = {}
        for sh in (1, 3, 2) if pieces[0] is not pieces[1] else (2, 1, 3):
            sent[sh] = send(pieces[sh - 1], axes, lambda q, sh=sh: q + sh)
        return [sent[sh] for sh in (1, 2, 3)]

    order = ("xy", "yz", "zx", "xy")
    swap = send(give, "cc", lambda q: 1 - q)
    acc = back_part(None, 0, 1)
    swap, acc = tie(swap, acc)
    m = part_rows // 8
    near_piece = ((m, out_chans), BF, near)
    y, *pieces = call(8, pair_kernel, [near_piece] * 4, [VM] * 2)(here(keep), here(swap))

    for ph, (lo, hi) in enumerate(((1, 4), (4, pairs), (pairs, pairs))):
        y, acc = tie(y, acc)
        got = shifts(order[ph], pieces)
        if lo < hi:
            acc = back_part(acc, lo, hi)
            *got, acc = tie(*got, acc)
        else:
            far = call(8, far_kernel, [((list_len, chans), BF, near)] * 4, [VM])(here(acc))
            returned = [
                lax.ppermute(far[0], "slab", down),
                lax.ppermute(far[1], "slab", up),
                lax.ppermute(far[2], "tile", chip),
                lax.ppermute(far[3], "tile", beside),
            ]
            g1, g2, g3, *returned = tie(*got, *returned)
            got = [g1, g2, g3]
        y = call(8, four_kernel, [near_piece], [VM] * 4)(*map(here, (y, *got)))
        pieces = [y] * 3

    got = shifts(order[3], [y] * 3)
    input_grad = call(
        12, add_kernel, [((row_count, chans), F32)], [VM] * 6, [pltpu.VMEM((far_rows, chans), BF)]
    )(here(acc), afar(boundary_rows), *map(here, returned))
    *got, input_grad = tie(*got, input_grad)
    full = call(8, join_kernel, [((4 * m, out_chans), BF, near)], [VM] * 4)(*map(here, (y, *got)))
    other = send(full, "cc", lambda q: 1 - q)
    conv_grad, down_grad = call(
        12,
        spread_kernel,
        [((kvol * BLOCK, out_chans), F32), ((child * BLOCK, out_chans), F32)],
        [VM, VM],
    )(here(full), here(other))
    return (
        coarse,
        input_grad,
        conv_grad.reshape(kvol, chans, chans),
        down_grad.reshape(child, chans, out_chans),
    )


def solution(mesh):
    return jax.shard_map(
        body,
        mesh=mesh,
        in_specs=(
            P(("slab", "tile"), None),
            P(),
            P(),
            P(("slab", "tile"), None),
            P(None, ("slab", "tile")),
            P(("slab", "tile"), None),
            P(("slab", "tile")),
        ),
        out_specs=(P(("slab", "tile"), None), P(("slab", "tile"), None), P(), P()),
        check_vma=False,
    )
```

```python
import functools

import jax
import jax.numpy as jnp
from jax import lax
from jax.experimental import pallas as pl
from jax.experimental.pallas import tpu as pltpu
from jax.sharding import PartitionSpec as P

BLOCK = 128
BF = jnp.bfloat16
F32 = jnp.float32
VM = pl.BlockSpec(memory_space=pltpu.VMEM)
SM = pl.BlockSpec(memory_space=pltpu.SMEM)

NN = (((1,), (0,)), ((), ()))
NT = (((1,), (1,)), ((), ()))
TN = (((0,), (0,)), ((), ()))


def mm(a, b, dims=NN):
    return lax.dot_general(a, b, dims, preferred_element_type=F32)


def sub_iota(rows, dtype=F32):
    return lax.broadcasted_iota(jnp.int32, (rows, BLOCK), 0).astype(F32).astype(dtype)


def onehot_t(row, ids):
    wide = jnp.broadcast_to(row, (16, BLOCK)).astype(BF)
    wide = jnp.concatenate([wide] * (ids.shape[0] // 16), axis=0)
    return jnp.where(ids == wide, jnp.ones((), BF), jnp.zeros((), BF))


def core_id():
    return lax.axis_index("tile") & 1


def list_order(core, rows_ref):
    rows = [rows_ref[d : d + 1, :] for d in range(4)]
    return (rows[0], rows[1], jnp.where(core == 0, rows[2], rows[3]), jnp.where(core == 0, rows[3], rows[2]))


def slot_order(core):
    return (0, 1, 3 - core, 2 + core)


def index_kernel(book_ref, code_ref, w_ref, dw_ref, cg_ref, src_ref, inner_ref, cell_ref, wt_ref, sg_ref):
    kvol = book_ref.shape[0]
    blocks, child, quarter = cell_ref.shape[0], 8, BLOCK // 4
    lane = lax.broadcasted_iota(jnp.int32, (kvol, BLOCK), 1)
    found = jnp.zeros((kvol, BLOCK), jnp.int32)
    for b in range(blocks):
        book = book_ref[:, b * BLOCK : (b + 1) * BLOCK]
        block = jnp.min(book, axis=1, keepdims=True) // BLOCK
        inner_ref[b] = (book - block * BLOCK).astype(F32)
        found = jnp.where(lane == b, block, found)
        code = code_ref[:, b * BLOCK : (b + 1) * BLOCK]
        cell = (code % child) * quarter + code // child - b * quarter
        cell_ref[b : b + 1, :] = jnp.where(code < child * quarter * blocks, cell, -1).astype(F32)
    src_ref[...] = found
    for k in range(kvol):
        wt_ref[:, k * BLOCK : (k + 1) * BLOCK] = w_ref[k].T
    for j in range(child):
        part = mm(cg_ref[...], dw_ref[j], NT).astype(BF)
        for b in range(blocks):
            sg_ref[b, j * quarter : (j + 1) * quarter, :] = part[b * quarter : (b + 1) * quarter, :]


def pick_kernel(feat_ref, rows_ref, *refs):
    out_refs, xt_ref, full_ref, hot_ref = refs[:-3], refs[-3], refs[-2], refs[-1]
    blocks = feat_ref.shape[0] // BLOCK
    length = rows_ref.shape[1]
    for b in range(blocks):
        block = feat_ref[b * BLOCK : (b + 1) * BLOCK, :].T
        xt_ref[b] = block
        full_ref[:, b * BLOCK : (b + 1) * BLOCK] = block
    ids = sub_iota(BLOCK, BF)
    for rows, out_ref in zip(list_order(core_id(), rows_ref), out_refs):
        for g in range(length // BLOCK):
            row = rows[:, g * BLOCK : (g + 1) * BLOCK]
            for b in range(blocks):
                hot_ref[b * BLOCK : (b + 1) * BLOCK, g * BLOCK : (g + 1) * BLOCK] = onehot_t(
                    (row - b * BLOCK).astype(F32), ids
                )
        out_ref[...] = mm(full_ref[...], hot_ref[...]).T.astype(BF)


def main_kernel(
    src_ref, xt_loc_ref, r0_ref, r1_ref, r2_ref, r3_ref, book_ref, cell_ref, wt_ref, sg_ref, dw_ref, cg_ref,
    coarse_ref, pg_ref, keep_ref, give_ref,
    xt_ref, gt_ref, ch_ref, part_ref,
):
    kvol = book_ref.shape[1]
    blocks = xt_loc_ref.shape[0]
    recv_refs = (r0_ref, r1_ref, r2_ref, r3_ref)
    each = r0_ref.shape[0] // BLOCK
    far = 4 * each
    child = dw_ref.shape[0]
    quarter = cg_ref.shape[0] // blocks
    ids = sub_iota(BLOCK, BF)
    ids2 = jnp.concatenate([ids, ids + jnp.asarray(BLOCK, BF)], axis=0)

    for b in range(blocks):
        xt_ref[b] = xt_loc_ref[b]
    for b in range(far):
        one = b % each
        slot = slot_order(core_id())[b // each]
        xt_ref[blocks + each * slot + one] = recv_refs[b // each][one * BLOCK : (one + 1) * BLOCK, :].T
    xt_ref[blocks + far] = jnp.zeros((BLOCK, BLOCK), BF)
    ch_ref[(blocks - 1) * quarter :, :] = jnp.zeros((quarter, child * BLOCK), BF)
    pg_ref[blocks // 2 - 1, BLOCK:, :] = jnp.zeros((BLOCK, BLOCK), BF)

    def some(p, count):
        for k in range(kvol):
            for h in range(count):
                b = 2 * p + h
                hot = onehot_t(book_ref[b, k : k + 1, :], ids)
                got = mm(xt_ref[src_ref[k, b]], hot)
                at = pl.multiple_of(p * 2 * BLOCK + h * BLOCK, BLOCK)
                gt_ref[k * BLOCK : (k + 1) * BLOCK, pl.ds(at, BLOCK)] = got.astype(BF)
        width = count * BLOCK
        pre = mm(wt_ref[...], gt_ref[:, pl.ds(pl.multiple_of(p * 2 * BLOCK, 2 * BLOCK), width)])
        hid = jnp.maximum(pre, 0.0).astype(BF)
        halves = []
        for h in range(count):
            b = 2 * p + h
            hot = onehot_t(cell_ref[pl.ds(b, 1), :], ids2)
            kids = mm(hot, hid[:, h * BLOCK : (h + 1) * BLOCK], NT).astype(BF)
            for j in range(child):
                ch_ref[pl.ds(pl.multiple_of(b * quarter, quarter), quarter), j * BLOCK : (j + 1) * BLOCK] = (
                    kids[j * quarter : (j + 1) * quarter, :]
                )
            halves.append(mm(sg_ref[b], hot, TN))
        grad = jnp.concatenate(halves, axis=1)
        pgt = jnp.where(pre > 0, grad, 0.0).astype(BF)
        pg_ref[p, 0:width, :] = pgt.T

    @pl.loop(0, blocks // 2 - 1)
    def _(p):
        some(p, 2)

    some(blocks // 2 - 1, 1)
    live = (blocks - 1) * BLOCK
    conv = mm(gt_ref[:, 0:live], pg_ref[...].reshape(blocks * BLOCK, BLOCK)[0:live, :])

    kids = ch_ref[...]
    coarse_ref[...] = mm(kids, dw_ref[...].reshape(child * BLOCK, BLOCK)).astype(BF)
    rows = kvol * BLOCK
    part_ref[0:rows, :] = conv.astype(BF)
    part_ref[rows : rows + child * BLOCK, :] = mm(kids, cg_ref[...], TN).astype(BF)
    rest = part_ref.shape[0] - rows - child * BLOCK
    part_ref[rows + child * BLOCK :, :] = jnp.zeros((rest, BLOCK), BF)
    half = keep_ref.shape[0]
    core = core_id()
    keep_ref[...] = part_ref[pl.ds(pl.multiple_of(core * half, half), half), :]
    give_ref[...] = part_ref[pl.ds(pl.multiple_of((1 - core) * half, half), half), :]


def back_kernel(lo, hi, pairs, src_ref, book_ref, wt_ref, pg_ref, *refs):
    *before_refs, table_ref, back_ref = refs
    table_ref[...] = jnp.zeros_like(table_ref) if lo == 0 else before_refs[0][...]
    kvol = book_ref.shape[1]
    ids = sub_iota(BLOCK, BF)

    def some(p, count):
        back_ref[0 : count * BLOCK, :] = mm(pg_ref[p, 0 : count * BLOCK, :], wt_ref[...]).astype(BF)
        for k in range(kvol):
            for h in range(count):
                b = 2 * p + h
                hot = onehot_t(book_ref[b, k : k + 1, :], ids)
                table_ref[src_ref[k, b]] += mm(
                    hot, back_ref[h * BLOCK : (h + 1) * BLOCK, k * BLOCK : (k + 1) * BLOCK]
                )

    @pl.loop(lo, min(hi, pairs - 1))
    def _(p):
        some(p, 2)

    if hi == pairs:
        some(pairs - 1, 1)


def far_kernel(table_ref, *far_refs):
    each = far_refs[0].shape[0] // BLOCK
    blocks = table_ref.shape[0] - 1 - 4 * each
    for slot, far_ref in zip(slot_order(core_id()), far_refs):
        for one in range(each):
            far_ref[one * BLOCK : (one + 1) * BLOCK, :] = table_ref[blocks + each * slot + one].astype(BF)


def add_rows(start, rows_ref, lists, ret_ref, out_ref):
    ids = sub_iota(BLOCK, BF)
    groups = [rows[:, g * BLOCK : (g + 1) * BLOCK] for rows in lists for g in range(rows_ref.shape[1] // BLOCK)]
    for b in range(out_ref.shape[0] // BLOCK):
        hot = jnp.concatenate([onehot_t((row - b * BLOCK).astype(F32), ids) for row in groups], axis=1)
        out_ref[b * BLOCK : (b + 1) * BLOCK, :] = start(b) + mm(hot, ret_ref[...])


def add_tile_kernel(table_ref, rows_ref, g2_ref, g3_ref, out_ref, ret_ref):
    length = rows_ref.shape[1]
    ret_ref[0:length, :] = g2_ref[...]
    ret_ref[length:, :] = g3_ref[...]
    add_rows(lambda b: table_ref[b], rows_ref, list_order(core_id(), rows_ref)[2:], ret_ref, out_ref)


def add_slab_kernel(part_ref, rows_ref, a0_ref, b0_ref, a1_ref, b1_ref, out_ref, ret_ref):
    length = rows_ref.shape[1]
    nothing = jnp.zeros((length, BLOCK), BF)
    slab = lax.axis_index("slab")
    first = core_id() == 0
    tail = pl.ds(a0_ref.shape[0] - length, length)
    above = jnp.where(first, a0_ref[tail, :], b0_ref[tail, :])
    below = jnp.where(first, a1_ref[tail, :], b1_ref[tail, :])
    ret_ref[0:length, :] = jnp.where(slab < lax.axis_size("slab") - 1, above, nothing)
    ret_ref[length:, :] = jnp.where(slab > 0, below, nothing)
    start = lambda b: part_ref[b * BLOCK : (b + 1) * BLOCK, :]
    add_rows(start, rows_ref, list_order(core_id(), rows_ref)[:2], ret_ref, out_ref)


def wide(v):
    return v.astype(F32)


def first_axis():
    return jnp.where(core_id() == 0, lax.axis_index("slab"), lax.axis_index("tile") >> 3)


def quarter_at(n, m):
    return pl.ds(pl.multiple_of((n & 3) * m, m), m)


def pair_kernel(keep_ref, swap_ref, mine_ref, *piece_refs):
    m = mine_ref.shape[0]
    place = first_axis()
    for sh, out_ref in enumerate((mine_ref, *piece_refs)):
        at = quarter_at(place + sh, m)
        out_ref[...] = (wide(keep_ref[at, :]) + wide(swap_ref[at, :])).astype(BF)


def four_kernel(own_ref, g1_ref, g2_ref, g3_ref, *refs):
    m = own_ref.shape[0]
    total = (wide(own_ref[...]) + wide(g2_ref[...])) + (wide(g1_ref[0:m, :]) + wide(g3_ref[0:m, :]))
    outs = refs[0:1] if len(refs) == 1 else refs[2:]
    for out_ref in outs:
        out_ref[0:m, :] = total.astype(BF)
    for out_ref, tail_ref in zip(outs[1:], refs):
        out_ref[m:, :] = tail_ref[...]


def join_kernel(own_ref, g1_ref, g2_ref, g3_ref, full_ref):
    m = own_ref.shape[0]
    place = first_axis() + 4
    for sh, ref in enumerate((own_ref, g1_ref, g2_ref, g3_ref)):
        full_ref[quarter_at(place - sh, m), :] = ref[0:m, :]


def spread_kernel(own_ref, other_ref, conv_ref, down_ref):
    half = own_ref.shape[0]
    rows = conv_ref.shape[0]

    def put(low_ref, high_ref):
        conv_ref[0:half, :] = low_ref[...].astype(F32)
        conv_ref[half:rows, :] = high_ref[0 : rows - half, :].astype(F32)
        down_ref[...] = high_ref[rows - half : rows - half + down_ref.shape[0], :].astype(F32)

    @pl.when(core_id() == 0)
    def _():
        put(own_ref, other_ref)

    @pl.when(core_id() != 0)
    def _():
        put(other_ref, own_ref)


def here(x):
    return pltpu.with_memory_space_constraint(x, pltpu.VMEM)


def afar(x):
    return pltpu.with_memory_space_constraint(x, pltpu.HBM)


def call(mib, kernel, outs, ins, scratch=()):
    single = len(outs) == 1
    shapes = tuple((jax.ShapeDtypeStruct if not near else pltpu.VMEM)(s, d) for s, d, *near in outs)
    return pl.pallas_call(
        kernel,
        out_shape=shapes[0] if single else shapes,
        in_specs=ins,
        out_specs=VM if single else tuple(VM for _ in outs),
        scratch_shapes=list(scratch),
        compiler_params=pltpu.CompilerParams(vmem_limit_bytes=mib * 1024 * 1024),
    )


def tie(*values):
    return lax.optimization_barrier(values)


def body(features, conv_weight, down_weight, coarse_grad, rulebook, boundary_rows, parent_code):
    row_count, chans = features.shape
    coarse_rows, out_chans = coarse_grad.shape
    list_len = boundary_rows.shape[1]
    child = down_weight.shape[0]
    kvol = conv_weight.shape[0]
    blocks = row_count // BLOCK
    pairs = blocks // 2
    far_rows = 4 * list_len
    quarter = coarse_rows // blocks
    slabs, tiles = lax.axis_size("slab"), lax.axis_size("tile")
    place = lax.axis_index("slab") * tiles + lax.axis_index("tile")
    core = place & 1

    near = True
    *outgoing, xt = call(
        12,
        pick_kernel,
        [((list_len, chans), BF, near)] * 4 + [((blocks, BLOCK, BLOCK), BF, near)],
        [VM, VM],
        [pltpu.VMEM((BLOCK, row_count), BF), pltpu.VMEM((row_count, list_len), BF)],
    )(afar(features), afar(boundary_rows))
    up = [(i, i + 1) for i in range(slabs - 1)]
    down = [(i + 1, i) for i in range(slabs - 1)]
    chip = [(i, i ^ 1) for i in range(tiles)]
    beside = [(i, i + 2 * (i % 2) - 1) for i in range(1, tiles - 1)]
    received = [
        lax.ppermute(outgoing[0], "slab", up),
        lax.ppermute(outgoing[1], "slab", down),
        lax.ppermute(outgoing[2], "tile", chip),
        lax.ppermute(outgoing[3], "tile", beside),
    ]
    source, inner, cell, wt, sg = call(
        12,
        index_kernel,
        [
            ((kvol, BLOCK), jnp.int32),
            ((blocks, kvol, BLOCK), F32, near),
            ((blocks, BLOCK), F32, near),
            ((BLOCK, kvol * BLOCK), BF, near),
            ((blocks, child * quarter, BLOCK), BF, near),
        ],
        [VM] * 5,
    )(*map(afar, (rulebook, parent_code.reshape(1, row_count), conv_weight, down_weight, coarse_grad)))

    grad_rows = (kvol + child) * BLOCK
    part_rows = -(-grad_rows // 512) * 512
    table = blocks + far_rows // BLOCK + 1
    coarse, pg, keep, give = call(
        32,
        main_kernel,
        [
            ((coarse_rows, out_chans), BF),
            ((pairs, 2 * BLOCK, BLOCK), BF, near),
            ((part_rows // 2, out_chans), BF, near),
            ((part_rows // 2, out_chans), BF, near),
        ],
        [SM] + [VM] * 11,
        [
            pltpu.VMEM((table, BLOCK, BLOCK), BF),
            pltpu.VMEM((kvol * BLOCK, row_count), BF),
            pltpu.VMEM((coarse_rows, child * BLOCK), BF),
            pltpu.VMEM((part_rows, BLOCK), BF),
        ],
    )(source, *map(here, (xt, *received, inner, cell, wt, sg)), afar(down_weight), afar(coarse_grad))

    def back_part(acc, lo, hi):
        ins = (source, here(inner), here(wt), here(pg)) + (() if acc is None else (here(acc),))
        return call(
            12,
            functools.partial(back_kernel, lo, hi, pairs),
            [((table, BLOCK, BLOCK), F32, near)],
            [SM] + [VM] * (len(ins) - 1),
            [pltpu.VMEM((2 * BLOCK, kvol * BLOCK), BF)],
        )(*ins)

    stride = {"c": 1, "z": 2, "y": 8, "x": tiles}
    size = {"c": 2, "z": 4, "y": tiles // 8, "x": slabs}

    def send(v, axes, to):
        links = []
        for i in range(slabs * tiles):
            axis = axes[i % 2]
            st, n = stride[axis], size[axis]
            q = (i // st) % n
            links.append((i, i + (to(q) % n - q) * st))
        return lax.ppermute(v, ("slab", "tile"), links)

    def shifts(axes, pieces):
        sent = {}
        for sh in (1, 3, 2) if pieces[0] is not pieces[1] else (2, 1, 3):
            sent[sh] = send(pieces[sh - 1], axes, lambda q, sh=sh: q + sh)
        return [sent[sh] for sh in (1, 2, 3)]

    order = ("xy", "yz", "zx", "xy")
    swap = send(give, "cc", lambda q: 1 - q)
    acc = back_part(None, 0, 1)
    swap, acc = tie(swap, acc)
    m = part_rows // 8
    near_piece = ((m, out_chans), BF, near)
    long_piece = ((m + list_len, out_chans), BF, near)
    y, *pieces = call(8, pair_kernel, [near_piece] * 4, [VM] * 2)(here(keep), here(swap))

    got = shifts(order[0], pieces)
    acc = back_part(acc, 1, 4)
    *got, acc = tie(*got, acc)
    y = call(8, four_kernel, [near_piece], [VM] * 4)(*map(here, (y, *got)))

    y, acc = tie(y, acc)
    got = shifts(order[1], [y] * 3)
    acc = back_part(acc, 4, pairs)
    far = call(8, far_kernel, [((list_len, chans), BF, near)] * 4, [VM])(here(acc))
    *got, far0, far1, far2, far3 = tie(*got, *far)

    longs = [near_piece, long_piece, long_piece]
    y, low, high = call(8, four_kernel, longs, [VM] * 6)(*map(here, (y, *got, far0, far1)))
    early = shifts(order[2], [high, y, low])
    beyond = lax.ppermute(far3, "tile", beside)
    across = lax.ppermute(far2, "tile", chip)
    *early, beyond, across = tie(*early, beyond, across)
    y, low, high = call(8, four_kernel, longs, [VM] * 6)(*map(here, (y, *early, far0, far1)))
    got = shifts(order[3], [high, y, low])
    part = call(
        12, add_tile_kernel, [((row_count, chans), F32, near)], [VM] * 4, [pltpu.VMEM((2 * list_len, chans), BF)]
    )(here(acc), afar(boundary_rows), here(across), here(beyond))
    *got, part = tie(*got, part)
    returned = [got[2], early[2], got[0], early[0]]
    full = call(8, join_kernel, [((4 * m, out_chans), BF, near)], [VM] * 4)(*map(here, (y, *got)))
    other = send(full, "cc", lambda q: 1 - q)
    input_grad = call(
        12, add_slab_kernel, [((row_count, chans), F32)], [VM] * 6, [pltpu.VMEM((2 * list_len, chans), BF)]
    )(here(part), afar(boundary_rows), *map(here, returned))
    other, input_grad = tie(other, input_grad)
    conv_grad, down_grad = call(
        12,
        spread_kernel,
        [((kvol * BLOCK, out_chans), F32), ((child * BLOCK, out_chans), F32)],
        [VM, VM],
    )(here(full), here(other))
    return (
        coarse,
        input_grad,
        conv_grad.reshape(kvol, chans, chans),
        down_grad.reshape(child, chans, out_chans),
    )


def solution(mesh):
    return jax.shard_map(
        body,
        mesh=mesh,
        in_specs=(
            P(("slab", "tile"), None),
            P(),
            P(),
            P(("slab", "tile"), None),
            P(None, ("slab", "tile")),
            P(("slab", "tile"), None),
            P(("slab", "tile")),
        ),
        out_specs=(P(("slab", "tile"), None), P(("slab", "tile"), None), P(), P()),
        check_vma=False,
    )
```
